128 devices in a mesh: section: 4 (over y_lo, core), dp: 16 (over z, x), mp: 2 (over y_hi).
Axes of the slice: x: 4, y: 4 (y_hi: 2, y_lo: 2; y = y_hi * 2 + y_lo), z: 4, core: 2. Of those that a mesh axis runs over, the one named last changes fastest.
Arguments:
- siglip_features: bfloat16 [8192, 1152], P('dp'), may hold values from -6 to 6
- convnext_features: bfloat16 [8192, 1536], P('dp'), may hold values from -6 to 6
- siglip_projection: bfloat16 [1152, 8192], P(None, ('section', 'mp')), may hold values from -0.125 to 0.125
- convnext_projection: bfloat16 [1536, 8192], P(None, ('section', 'mp')), may hold values from -0.125 to 0.125
- newline_embed: bfloat16 [8192], P(('section', 'mp')), may hold values from -6 to 6
- key_value_weight: bfloat16 [2048, 8192], P(None, ('section', 'mp')), may hold values from -0.0625 to 0.0625
- tile_rank: int32 [256, 1], replicated, may hold values from 0 to 15; in each aligned block of 16 rows (0 to 15, 16 to 31, ...) at most 2 rows name the same one
- row_end: int32 [256], replicated, may hold values 0 or 1
- key_value_grad: bfloat16 [16384, 2048], P('dp'), may hold values from -0.059814453 to 0.059814453
- newline_grad: bfloat16 [512, 2048], P('dp'), may hold values from -1.796875 to 1.796875
Outputs:
- siglip_weight_grad: float32 [1152, 8192], P('dp', ('section', 'mp'))
- convnext_weight_grad: float32 [1536, 8192], P('dp', ('section', 'mp'))
- key_value_weight_grad: float32 [2048, 8192], P('dp', ('section', 'mp'))
The draws below stay inside these ranges and needn't reach their ends.
Inputs may be any that keep to these rules, and one draw needn't show every extreme that they name: `tile_rank`: each aligned block of 16 tiles (the tiles of one index of dp) sends at most 2 tiles to one rank, and exactly 2 to some rank.
All inputs are finite; a program needn't handle non-finite values.
Results may differ from the reference program's by a relative error of at most 0.007.
Values may be sent and summed in bfloat16 or wider, within the bound.
No kernel may reach another device: no remote copies, remote signals or barrier semaphores. Data moves between devices by JAX's collectives and lax.ppermute only.
A program may use at most 128 MiB of HBM per device.

```python
import math
import jax
import jax.numpy as jnp
import numpy as np
from jax import lax

D = 8192
SIG = 1152
CONV = 1536
TT = 32
TILE_DEV = 16
KV = 1024
CAP = 2
TILES = 256
SLOTS = 32
TOKENS = 8192
N_DP = 16


def plant(values, key, smallest, top_value):
    dims = values.shape
    place = [jax.random.randint(jax.random.fold_in(key, axis), (), 0, dims[axis]) for axis in range(len(dims))]
    values = values.at[tuple(place)].set(smallest)
    longest = dims.index(max(dims))
    place[longest] = (place[longest] + 1) % dims[longest]
    return values.at[tuple(place)].set(top_value)


def raised(drawn, rng, source, target, blocks, factor):
    def block_of(axis_at):
        return (jnp.arange(drawn.shape[axis_at]) // (drawn.shape[axis_at] // blocks)).reshape((-1,) + (1,) * (drawn.ndim - 1 - axis_at))

    first = jax.random.permutation(rng, blocks)[block_of(target)]
    far = (block_of(target) + blocks // 2) % blocks
    return jnp.where((block_of(source) == first) | (block_of(source) == far), factor * drawn, drawn)


def block_levels(key, dims, pieces, least, top_value):
    gain, own = 1.0, jax.random.fold_in(key, 6)
    for position, blocks in pieces:
        heights = jnp.exp(jax.random.uniform(jax.random.fold_in(own, position), (blocks,), jnp.float32, least / len(pieces), top_value / len(pieces)))
        gain = gain * jnp.repeat(heights, dims[position] // blocks).reshape([-1 if axis == position else 1 for axis in range(len(dims))])
    return gain


def assign_block(rng, own, number, rows, number_of, top, most, skew):
    sequence = jax.random.permutation(rng, number_of)
    packed, ordinary = portions_of(number_of, rows * top, most, skew, True), portions_of(number_of, rows * top, most, skew, False)
    places = jnp.arange(number_of)

    def named(sizes, rotation):
        used = int((sizes > 0).sum())
        fixed = max(1, used // 4)
        moved = fixed + (places - fixed + rotation * (used - fixed)) % max(1, number_of - fixed)
        return jnp.zeros((number_of,), jnp.int32).at[sequence[jnp.where(places < fixed, places, moved)]].set(jnp.asarray(sizes, jnp.int32))

    sizes = jnp.where(number % 4 == 0, named(packed, number // 4), named(ordinary, number - number // 4 - 1))
    mixed = jax.random.permutation(jax.random.fold_in(own, 3), number_of)
    giver, taker = mixed[0:number_of // 2 * 2:2], mixed[1:number_of // 2 * 2:2]
    slack = jnp.minimum(sizes[giver] - 1, most - sizes[taker]) // 2
    slack = jnp.where((giver == sequence[0]) | (taker == sequence[0]) | (sizes[taker] == 0), 0, jnp.maximum(slack, 0))
    moved = jax.random.randint(jax.random.fold_in(own, 4), (number_of // 2,), 0, 1 << 20) % (slack + 1)
    sizes = sizes.at[giver].add(-moved).at[taker].add(moved)
    members = jnp.searchsorted(jnp.cumsum(sizes), jnp.arange(rows * top), side="right").astype(jnp.int32)
    table = members.reshape(top, rows).T
    table = table[jax.random.permutation(jax.random.fold_in(own, 1), rows)]
    rotation = jax.random.randint(jax.random.fold_in(own, 2), (rows, 1), 0, top)
    return jnp.take_along_axis(table, (jnp.arange(top)[None, :] + rotation) % top, axis=1)


def portions_of(count, total, limit, slope, full):
    weights = [(1 << 20) // math.isqrt(grade ** slope) + 1 for grade in range(1, count + 1)]
    largest = limit if full else min(limit, max(-(-total // count), total * weights[0] // sum(weights)))
    least = 1 if total - largest >= count - 1 else 0
    holding, surplus = [largest] + [least] * (count - 1), total - largest - least * (count - 1)
    while surplus > 0:
        free = [i for i in range(1, count) if holding[i] < largest] or [i for i in range(1, count) if holding[i] < limit]
        mass, left = sum([weights[i] for i in free]), surplus
        for i in free:
            addition = min(limit - holding[i], max(1, left * weights[i] // mass), surplus)
            holding[i] = holding[i] + addition
            surplus = surplus - addition
    return np.array(holding)


def noise(key, extent, deviation, most, cuts=(), kind=jnp.bfloat16):
    level = block_levels(key, extent, cuts, -0.22, 0.18) if cuts else 1.0
    values = jax.random.normal(key, extent, jnp.float32) * deviation * level
    return jnp.minimum(jnp.maximum(values, -most), most).astype(kind)


def bell_draw_with(key, shape, width, reach, pieces, heavy, kind=jnp.bfloat16):
    drawn = width * jax.random.normal(key, shape, jnp.float32)
    if pieces:
        drawn = drawn * block_levels(key, shape, pieces, -0.22, 0.18)
    return jnp.clip(raised(drawn, jax.random.fold_in(key, 3), *heavy), -reach, reach).astype(kind)


def setup_inputs(seed: int = 0) -> dict:
    seeds = jax.random.split(jax.random.key(seed), 11)
    siglip_features = bell_draw_with(seeds[0], (TOKENS, SIG), 1.0, 6.0, ((0, 16),), (0, 1, 16, 2.0))
    convnext_features = bell_draw_with(seeds[1], (TOKENS, CONV), 1.0, 6.0, ((0, 16),), (0, 1, 16, 2.0))
    siglip_projection = noise(seeds[2], (SIG, D), (SIG + CONV) ** -0.5, 0.125, ((1, 8),))
    convnext_projection = noise(seeds[3], (CONV, D), (SIG + CONV) ** -0.5, 0.125, ((1, 8),))
    newline_embed = noise(seeds[4], (D,), 1.0, 6.0, ((0, 8),))
    key_value_weight = noise(seeds[5], (2 * KV, D), D ** -0.5, 0.0625, ((1, 8),))
    tile_rank_keys = jax.random.split(jax.random.fold_in(seeds[6], 1), TILES // TILE_DEV)
    tile_rank_turns = jax.random.permutation(jax.random.fold_in(seeds[6], 3), TILES // TILE_DEV)
    tile_rank = jax.vmap(lambda own, number: assign_block(jax.random.fold_in(seeds[6], 2), own, number, TILE_DEV, N_DP, 1, CAP, 2))(tile_rank_keys, tile_rank_turns).reshape((TILES, 1))
    row_end = plant((jax.random.randint(seeds[7], (TILES,), 0, 3) < 1).astype(jnp.int32), jax.random.fold_in(seeds[7], 1), 0, 1)
    key_value_grad = bell_draw_with(seeds[8], (N_DP * SLOTS * TT, 2 * KV), 0.01, 0.059814453, ((0, 16),), (0, 1, 16, 2.0))
    newline_grad = noise(seeds[9], (N_DP * SLOTS, 2 * KV), 0.3, 1.796875, ((0, 16),))
    return dict(siglip_features=siglip_features, convnext_features=convnext_features, siglip_projection=siglip_projection, convnext_projection=convnext_projection, newline_embed=newline_embed, key_value_weight=key_value_weight, tile_rank=tile_rank, row_end=row_end, key_value_grad=key_value_grad, newline_grad=newline_grad)


epsilon = 1e-06

def tile_slots(tile_rank):
    dest_rank = tile_rank[:, 0].astype(jnp.int32)
    tile_count = dest_rank.shape[0]
    per_device = tile_count // N_DP
    onehot = (dest_rank[:, None] == jnp.arange(N_DP, dtype=jnp.int32)[None, :]).astype(jnp.int32)
    blocks = onehot.reshape(N_DP, per_device, N_DP)
    before = jnp.cumsum(blocks, axis=1) - blocks
    slot_place = lax.optimization_barrier(jnp.sum(before * blocks, axis=2)).reshape(tile_count).astype(jnp.int32)
    source = (jnp.arange(tile_count, dtype=jnp.int32) // per_device).astype(jnp.int32)
    return ((dest_rank * N_DP + source) * CAP + slot_place).astype(jnp.int32)

def reference(siglip_features, convnext_features, siglip_projection, convnext_projection, newline_embed, key_value_weight, tile_rank, row_end, key_value_grad, newline_grad):
    slot_index = tile_slots(tile_rank)
    projected = (jnp.dot(siglip_features, siglip_projection, preferred_element_type=jnp.float32) + jnp.dot(convnext_features, convnext_projection, preferred_element_type=jnp.float32)).astype(jnp.bfloat16)
    proj_values = projected.astype(jnp.float32)
    inverse_rms = lax.rsqrt(lax.optimization_barrier(jnp.mean(proj_values * proj_values, axis=1, keepdims=True)) + epsilon)
    normed = (proj_values * inverse_rms).astype(jnp.bfloat16)
    line_vector = newline_embed.astype(jnp.float32)
    line_normed = (line_vector * lax.rsqrt(jnp.mean(line_vector * line_vector) + epsilon)).astype(jnp.bfloat16)
    tile_grads = key_value_grad.reshape(N_DP * SLOTS, TT, 2 * KV)[slot_index].reshape(TILES * TT, 2 * KV)
    kv_term = jnp.dot(tile_grads.T, normed, preferred_element_type=jnp.float32)
    line_rows = newline_grad[slot_index].astype(jnp.float32) * row_end.astype(jnp.float32)[:, None]
    line_total = lax.optimization_barrier(jnp.sum(line_rows, axis=0))
    key_value_weight_grad = kv_term + line_total[:, None] * line_normed.astype(jnp.float32)[None, :]
    normed_grad = jnp.dot(tile_grads, key_value_weight, preferred_element_type=jnp.float32).astype(jnp.bfloat16)
    grad_values = normed_grad.astype(jnp.float32)
    products = lax.optimization_barrier(jnp.sum(grad_values * proj_values, axis=1, keepdims=True))
    projected_grad = (inverse_rms * grad_values - inverse_rms ** 3 * proj_values * products / D).astype(jnp.bfloat16)
    siglip_weight_grad = jnp.dot(siglip_features.T, projected_grad, preferred_element_type=jnp.float32)
    convnext_weight_grad = jnp.dot(convnext_features.T, projected_grad, preferred_element_type=jnp.float32)
    return (siglip_weight_grad, convnext_weight_grad, key_value_weight_grad)
```

```python
import jax
import jax.numpy as jnp
from jax import lax
from jax.experimental import pallas as pl
from jax.experimental.pallas import tpu as pltpu
from jax.sharding import Mesh, PartitionSpec as P

D = 8192
epsilon = 1e-06
N = 4
TT = 32
CAP = 2
BF = jnp.bfloat16
F32 = jnp.float32
DP = ("z", "x")
Y = ("ylo", "yhi")


def shift(value, axis, size, step):
    return lax.ppermute(value, axis, [(i, (i + step) % size) for i in range(size)])


def shift_y(value, step):
    place = lambda y: (y % 2) * 2 + y // 2
    return lax.ppermute(value, Y, [(place(y), place((y + step) % N)) for y in range(N)])


def all_sum(value):
    value = value + shift(value, "core", 2, 1)
    parts = [shift_y(value, step) for step in (1, 2, 3)]
    return value + parts[0] + parts[1] + parts[2]


def slices_out(key_value_grad, member):
    blocks = N * N
    rows = key_value_grad.shape[0] // blocks
    width = key_value_grad.shape[1] // blocks

    def kernel(member_ref, source, out, sems):
        me = member_ref[0]
        copies = []
        for dest in range(blocks):
            for part in range(2):
                place = 2 * me + part
                dx, dz = place // N, place % N
                column = ((dest // N + dz) % N) * N + (dest % N + dx) % N
                copy = pltpu.make_async_copy(
                    source.at[pl.ds(dest * rows, rows), pl.ds(pl.multiple_of(column * width, width), width)],
                    out.at[dest, :, pl.ds(part * width, width)],
                    sems.at[dest * 2 + part],
                )
                copy.start()
                copies.append(copy)
        for copy in copies:
            copy.wait()

    return pl.pallas_call(
        kernel,
        out_shape=jax.ShapeDtypeStruct((blocks, rows, 2 * width), key_value_grad.dtype),
        grid_spec=pltpu.PrefetchScalarGridSpec(
            num_scalar_prefetch=1,
            grid=(1,),
            in_specs=[pl.BlockSpec(memory_space=pl.ANY)],
            out_specs=pl.BlockSpec(memory_space=pl.ANY),
            scratch_shapes=[pltpu.SemaphoreType.DMA((2 * blocks,))],
        ),
        name="slices_out",
    )(member, key_value_grad)


def block_order(source, table):
    count = table.shape[0]

    def kernel(table_ref, source_ref, out, sems):
        copies = []
        for i in range(count):
            copy = pltpu.make_async_copy(source_ref.at[table_ref[i]], out.at[i], sems.at[i])
            copy.start()
            copies.append(copy)
        for copy in copies:
            copy.wait()

    return pl.pallas_call(
        kernel,
        out_shape=jax.ShapeDtypeStruct((count,) + source.shape[1:], source.dtype),
        grid_spec=pltpu.PrefetchScalarGridSpec(
            num_scalar_prefetch=1,
            grid=(1,),
            in_specs=[pl.BlockSpec(memory_space=pl.ANY)],
            out_specs=pl.BlockSpec(memory_space=pl.ANY),
            scratch_shapes=[pltpu.SemaphoreType.DMA((count,))],
        ),
        name="block_order",
    )(table, source)


def pick_tiles(received, dests):
    tiles = dests.shape[0]
    slots, _, width = received.shape

    def kernel(dest_ref, source, out):
        names = [dest_ref[j] for j in range(tiles)]
        for j in range(tiles):
            before = jnp.int32(0)
            for i in range(j):
                before = before + (names[i] == names[j]).astype(jnp.int32)
            out[j] = source[names[j] * CAP + before]

    return pl.pallas_call(
        kernel,
        out_shape=jax.ShapeDtypeStruct((tiles, TT, width), received.dtype),
        grid_spec=pltpu.PrefetchScalarGridSpec(
            num_scalar_prefetch=1,
            grid=(1,),
            in_specs=[pl.BlockSpec((slots, TT, width), lambda i, t: (0, 0, 0))],
            out_specs=pl.BlockSpec((tiles, TT, width), lambda i, t: (0, 0, 0)),
        ),
        name="pick_tiles",
    )(dests, received)


def assemble(pieces, places):
    rows, wide = pieces[0].shape
    width = wide // 2
    count = len(pieces)

    def kernel(place_ref, *refs):
        sources, first, second = refs[:count], refs[count], refs[count + 1]
        for p in range(count):
            for part in range(2):
                place = 2 * place_ref[p] + part
                other = (place % N) * N + place // N
                value = sources[p][:, part * width:(part + 1) * width]
                first[:, pl.ds(pl.multiple_of(place * width, width), width)] = value
                second[:, pl.ds(pl.multiple_of(other * width, width), width)] = value

    shape = jax.ShapeDtypeStruct((rows, wide * count), pieces[0].dtype)
    whole = pl.BlockSpec((rows, wide * count), lambda i, t: (0, 0))
    return pl.pallas_call(
        kernel,
        out_shape=(shape, shape),
        grid_spec=pltpu.PrefetchScalarGridSpec(
            num_scalar_prefetch=1,
            grid=(1,),
            in_specs=[pl.BlockSpec((rows, wide), lambda i, t: (0, 0))] * count,
            out_specs=(whole, whole),
        ),
        compiler_params=pltpu.CompilerParams(vmem_limit_bytes=40 * 1024 * 1024),
        name="assemble",
    )(places, *pieces)


def reduce_scatter(piece, first, second, rows, part):
    big = N * rows
    half = 2 * rows
    down = rows - part
    ahead = shift(piece(big + half, big).astype(BF), first, N, 1)
    behind = shift(piece(2 * big + half, big).astype(BF), first, N, 3)
    ahead2 = shift((piece(big, half) + ahead[half:].astype(F32)).astype(BF), first, N, 1)
    behind2 = shift((piece(3 * big + half, half) + behind[:half].astype(F32)).astype(BF), first, N, 3)

    def low(start, stop):
        return (
            piece(start, stop - start)
            + behind[half + start:half + stop].astype(F32)
            + ahead2[start:stop].astype(F32)
        )

    def high(start, stop):
        return (
            piece(start, stop - start)
            + ahead[start - half:stop - half].astype(F32)
            + behind2[start - half:stop - half].astype(F32)
        )

    send_a = jnp.concatenate(
        [low(rows + part, half).astype(BF), high(half, half + part).astype(BF)], axis=0
    )
    send_b = high(half + part, half + rows + part).astype(BF)
    ahead3 = shift(send_a, second, N, 1)
    behind3 = shift(send_b, second, N, 3)
    ahead4 = shift((low(rows, rows + part) + ahead3[down:].astype(F32)).astype(BF), second, N, 1)
    behind4 = shift(
        (high(half + rows + part, big) + behind3[:down].astype(F32)).astype(BF), second, N, 3
    )
    top = low(0, part) + behind3[down:].astype(F32) + ahead4.astype(F32)
    bottom = low(part, rows) + ahead3[:down].astype(F32) + behind4.astype(F32)
    return jnp.concatenate([top, bottom], axis=0)


def local(
    siglip_features,
    convnext_features,
    siglip_projection,
    convnext_projection,
    newline_embed,
    key_value_weight,
    tile_rank,
    row_end,
    key_value_grad,
    newline_grad,
):
    blocks = N * N
    z, x = lax.axis_index("z"), lax.axis_index("x")
    ylo, core, yhi = lax.axis_index("ylo"), lax.axis_index("core"), lax.axis_index("yhi")
    my_rank = z * N + x
    member = (ylo * 2 + core) * 2 + yhi
    tiles = tile_rank.shape[0]
    per_device = tiles // blocks
    rows = siglip_features.shape[0]
    share = siglip_projection.shape[1]
    half = share // 2
    kv_rows = key_value_weight.shape[0] // blocks
    sig_rows = siglip_features.shape[1] // blocks
    conv_rows = convnext_features.shape[1] // blocks

    dest_rank = tile_rank.reshape(tiles)
    mine = lax.dynamic_slice_in_dim(dest_rank, my_rank * per_device, per_device)
    outgoing = slices_out(key_value_grad, member.reshape(1).astype(jnp.int32))
    received = lax.all_to_all(outgoing, DP, split_axis=0, concat_axis=0, tiled=True)

    projected = (
        jnp.dot(siglip_features, siglip_projection, preferred_element_type=F32)
        + jnp.dot(convnext_features, convnext_projection, preferred_element_type=F32)
    ).astype(BF)
    proj_values = projected.astype(F32)
    line_vector = newline_embed.astype(F32)
    squares = jnp.sum(proj_values * proj_values, axis=1).reshape(rows // 128, 128)
    line_square = jnp.broadcast_to(jnp.sum(line_vector * line_vector), (4, 128))
    statistic = all_sum(jnp.concatenate([squares, line_square], axis=0))
    inverse = lax.rsqrt(statistic[: rows // 128].reshape(rows) / D + epsilon)[:, None]
    line_normed = (line_vector * lax.rsqrt(statistic[rows // 128, 0] / D + epsilon)).astype(BF).astype(F32)
    normed = (proj_values * inverse).astype(BF)

    step = jnp.arange(blocks, dtype=jnp.int32)
    outer, inner = step // N, step % N
    table1 = ((z + inner) % N) * N + (x + outer) % N
    table2 = ((z + outer) % N) * N + (x + inner) % N
    features = jnp.concatenate(
        [
            siglip_features.T.reshape(blocks, sig_rows, rows),
            convnext_features.T.reshape(blocks, conv_rows, rows),
        ],
        axis=1,
    )
    x_rows = sig_rows + conv_rows
    features1 = block_order(features, table1).reshape(blocks * x_rows, rows)
    features2 = block_order(features, table2).reshape(blocks * x_rows, rows)
    weight = block_order(key_value_weight.reshape(blocks, kv_rows, share), table1).reshape(
        blocks * kv_rows, share
    )

    onehot = (dest_rank[:, None] == jnp.arange(blocks, dtype=jnp.int32)[None, :]).astype(jnp.int32)
    grouped = onehot.reshape(blocks, per_device, blocks)
    before = jnp.cumsum(grouped, axis=1) - grouped
    slot_place = jnp.sum(before * grouped, axis=2).reshape(tiles)
    slot = (jnp.arange(tiles, dtype=jnp.int32) // per_device) * CAP + slot_place
    live = (dest_rank == my_rank) & (row_end == 1)
    mask = jnp.sum(
        ((slot[:, None] == jnp.arange(blocks * CAP, dtype=jnp.int32)[None, :]) & live[:, None]).astype(
            jnp.int32
        ),
        axis=0,
    )
    line_total = jnp.dot(mask.astype(BF)[None, :], newline_grad, preferred_element_type=F32)[0]
    line_blocks = line_total.reshape(blocks, kv_rows)
    line1 = line_blocks[table1].reshape(blocks * kv_rows)[:, None]
    line2 = line_blocks[table2].reshape(blocks * kv_rows)[:, None]

    own = pick_tiles(received.reshape(blocks * CAP, TT, received.shape[2]), mine).reshape(
        rows, received.shape[2]
    )
    ring = [own] + [shift_y(own, s) for s in (1, 3, 2)]
    pieces = ring + [shift(piece, "core", 2, 1) for piece in ring]
    places = []
    y = yhi * 2 + ylo
    for side in (0, 1):
        for s in (0, 1, 3, 2):
            other = (y - s) % N
            places.append(((other % 2) * 2 + (core + side) % 2) * 2 + other // 2)
    grads1, grads2 = assemble(pieces, jnp.stack(places).astype(jnp.int32))

    def kv_piece(grads, line, columns):
        right = normed[:, columns]
        across = line_normed[None, columns]

        def piece(start, count):
            return (
                lax.dot_general(
                    grads[:, start:start + count],
                    right,
                    (((0,), (0,)), ((), ())),
                    preferred_element_type=F32,
                )
                + line[start:start + count] * across
            )

        return piece

    left, right = slice(0, half), slice(half, share)
    kv_result = jnp.concatenate(
        [
            reduce_scatter(kv_piece(grads1, line1, left), "x", "z", kv_rows, kv_rows // 2),
            reduce_scatter(kv_piece(grads2, line2, right), "z", "x", kv_rows, kv_rows // 2),
        ],
        axis=1,
    )

    grad_values = jnp.dot(grads1, weight, preferred_element_type=F32).astype(BF).astype(F32)
    products = all_sum(jnp.sum(grad_values * proj_values, axis=1).reshape(rows // 128, 128))
    products = products.reshape(rows)[:, None]
    projected_grad = (
        inverse * grad_values - inverse**3 * proj_values * products / D
    ).astype(BF)

    def x_piece(lhs, columns):
        right = projected_grad[:, columns]

        def piece(start, count):
            return jnp.dot(lhs[start:start + count], right, preferred_element_type=F32)

        return piece

    part = (x_rows // 2 + 7) // 8 * 8
    x_result = jnp.concatenate(
        [
            reduce_scatter(x_piece(features1, left), "x", "z", x_rows, part),
            reduce_scatter(x_piece(features2, right), "z", "x", x_rows, part),
        ],
        axis=1,
    )
    return x_result[:sig_rows], x_result[sig_rows:], kv_result


def solution(mesh):
    fine = Mesh(mesh.devices.reshape(2, 2, N, N, 2), ("ylo", "core", "z", "x", "yhi"))
    wide = ("ylo", "core", "yhi")
    in_specs = (
        P(DP, None),
        P(DP, None),
        P(None, wide),
        P(None, wide),
        P(wide),
        P(None, wide),
        P(),
        P(),
        P(DP, None),
        P(DP, None),
    )
    out_specs = (P(DP, wide), P(DP, wide), P(DP, wide))
    return jax.shard_map(local, mesh=fine, in_specs=in_specs, out_specs=out_specs, check_vma=False)
```

```python
import jax
import jax.numpy as jnp
from jax import lax
from jax.experimental import pallas as pl
from jax.experimental.pallas import tpu as pltpu
from jax.sharding import Mesh, PartitionSpec as P

D = 8192
epsilon = 1e-06
N = 4
TT = 32
CAP = 2
BF = jnp.bfloat16
F32 = jnp.float32
DP = ("z", "x")
Y = ("ylo", "yhi")


def shift(value, axis, size, step):
    return lax.ppermute(value, axis, [(i, (i + step) % size) for i in range(size)])


def shift_y(value, step):
    place = lambda y: (y % 2) * 2 + y // 2
    return lax.ppermute(value, Y, [(place(y), place((y + step) % N)) for y in range(N)])


def all_sum(value):
    value = value + shift(value, "core", 2, 1)
    parts = [shift_y(value, step) for step in (1, 2, 3)]
    return value + parts[0] + parts[1] + parts[2]


def slices_out(key_value_grad, member):
    blocks = N * N
    rows = key_value_grad.shape[0] // blocks
    width = key_value_grad.shape[1] // blocks

    def kernel(member_ref, source, out, sems):
        me = member_ref[0]
        copies = []
        for dest in range(blocks):
            for part in range(2):
                place = 2 * me + part
                dx, dz = place // N, place % N
                column = ((dest // N + dz) % N) * N + (dest % N + dx) % N
                copy = pltpu.make_async_copy(
                    source.at[pl.ds(dest * rows, rows), pl.ds(pl.multiple_of(column * width, width), width)],
                    out.at[dest, :, pl.ds(part * width, width)],
                    sems.at[dest * 2 + part],
                )
                copy.start()
                copies.append(copy)
        for copy in copies:
            copy.wait()

    return pl.pallas_call(
        kernel,
        out_shape=jax.ShapeDtypeStruct((blocks, rows, 2 * width), key_value_grad.dtype),
        grid_spec=pltpu.PrefetchScalarGridSpec(
            num_scalar_prefetch=1,
            grid=(1,),
            in_specs=[pl.BlockSpec(memory_space=pl.ANY)],
            out_specs=pl.BlockSpec(memory_space=pltpu.VMEM),
            scratch_shapes=[pltpu.SemaphoreType.DMA((2 * blocks,))],
        ),
        name="slices_out",
    )(member, key_value_grad)


CUTS = ((6, 10), (10, 14), (4, 6), (14, 16), (0, 4))


def cut_orders(source, tables):
    blocks, rows, width = source.shape
    orders = tables.shape[0] // blocks

    def kernel(table_ref, source_ref, *outs):
        for order in range(orders):
            for piece, (start, stop) in enumerate(CUTS):
                out = outs[order * len(CUTS) + piece]
                for i in range(start, stop):
                    out[(i - start) * rows:(i - start + 1) * rows] = source_ref[table_ref[order * blocks + i]]

    shapes = [jax.ShapeDtypeStruct(((stop - start) * rows, width), source.dtype) for start, stop in CUTS] * orders
    outs = pl.pallas_call(
        kernel,
        out_shape=shapes,
        grid_spec=pltpu.PrefetchScalarGridSpec(
            num_scalar_prefetch=1,
            grid=(1,),
            in_specs=[pl.BlockSpec(source.shape, lambda i, t: (0, 0, 0))],
            out_specs=[pl.BlockSpec(shape.shape, lambda i, t: (0, 0)) for shape in shapes],
        ),
        compiler_params=pltpu.CompilerParams(vmem_limit_bytes=40 * 1024 * 1024),
        name="cut_orders",
    )(tables, source)
    return [outs[order * len(CUTS):(order + 1) * len(CUTS)] for order in range(orders)]


def block_order(source, table):
    count = table.shape[0]

    def kernel(table_ref, source_ref, out, sems):
        copies = []
        for i in range(count):
            copy = pltpu.make_async_copy(source_ref.at[table_ref[i]], out.at[i], sems.at[i])
            copy.start()
            copies.append(copy)
        for copy in copies:
            copy.wait()

    return pl.pallas_call(
        kernel,
        out_shape=jax.ShapeDtypeStruct((count,) + source.shape[1:], source.dtype),
        grid_spec=pltpu.PrefetchScalarGridSpec(
            num_scalar_prefetch=1,
            grid=(1,),
            in_specs=[pl.BlockSpec(memory_space=pl.ANY)],
            out_specs=pl.BlockSpec(memory_space=pltpu.VMEM),
            scratch_shapes=[pltpu.SemaphoreType.DMA((count,))],
        ),
        compiler_params=pltpu.CompilerParams(vmem_limit_bytes=16 * 1024 * 1024),
        name="block_order",
    )(table, source)


def pick_tiles(received, dests):
    tiles = dests.shape[0]
    slots, _, width = received.shape

    def kernel(dest_ref, source, out):
        names = [dest_ref[j] for j in range(tiles)]
        for j in range(tiles):
            before = jnp.int32(0)
            for i in range(j):
                before = before + (names[i] == names[j]).astype(jnp.int32)
            out[j] = source[names[j] * CAP + before]

    return pl.pallas_call(
        kernel,
        out_shape=jax.ShapeDtypeStruct((tiles, TT, width), received.dtype),
        grid_spec=pltpu.PrefetchScalarGridSpec(
            num_scalar_prefetch=1,
            grid=(1,),
            in_specs=[pl.BlockSpec((slots, TT, width), lambda i, t: (0, 0, 0))],
            out_specs=pl.BlockSpec((tiles, TT, width), lambda i, t: (0, 0, 0)),
        ),
        name="pick_tiles",
    )(dests, received)


def assemble(pieces, places):
    rows, wide = pieces[0].shape
    width = wide // 2
    count = len(pieces)

    def kernel(place_ref, *refs):
        sources = refs[:count]
        whole = refs[count]
        cuts = refs[count + 1:count + 1 + 2 * len(CUTS)]
        second = refs[-1]
        for p in range(count):
            for part in range(2):
                place = 2 * place_ref[p] + part
                other = (place % N) * N + place // N
                value = sources[p][:, part * width:(part + 1) * width]
                whole[:, pl.ds(pl.multiple_of(place * width, width), width)] = value
                second[:, pl.ds(pl.multiple_of(other * width, width), width)] = value
        for order, source in enumerate((whole, second)):
            for piece, (start, stop) in enumerate(CUTS):
                cuts[order * len(CUTS) + piece][...] = source[:, start * width:stop * width]

    dtype = pieces[0].dtype
    shapes = [jax.ShapeDtypeStruct((rows, wide * count), dtype)] + [
        jax.ShapeDtypeStruct((rows, (stop - start) * width), dtype) for start, stop in CUTS
    ] * 2
    outs = pl.pallas_call(
        kernel,
        out_shape=shapes,
        grid_spec=pltpu.PrefetchScalarGridSpec(
            num_scalar_prefetch=1,
            grid=(1,),
            in_specs=[pl.BlockSpec((rows, wide), lambda i, t: (0, 0))] * count,
            out_specs=[pl.BlockSpec(shape.shape, lambda i, t: (0, 0)) for shape in shapes],
            scratch_shapes=[pltpu.VMEM((rows, wide * count), dtype)],
        ),
        compiler_params=pltpu.CompilerParams(vmem_limit_bytes=40 * 1024 * 1024),
        name="assemble",
    )(places, *pieces)
    return outs[0], outs[1:1 + len(CUTS)], outs[1 + len(CUTS):]


class Sums:
    def __init__(self, pieces, rows, part):
        self.pieces, self.rows, self.part = pieces, rows, part
        self.half, self.down = 2 * rows, rows - part

    def first_a(self):
        return self.pieces[0]().astype(BF), self.pieces[1]().astype(BF)

    def first_b(self, ahead, behind):
        self.ahead, self.behind = ahead.astype(F32), behind.astype(F32)
        return (
            (self.pieces[2]() + self.ahead[self.half:]).astype(BF),
            (self.pieces[3]() + self.behind[:self.half]).astype(BF),
        )

    def second_a(self, ahead, behind):
        half, rows, part = self.half, self.rows, self.part
        own = self.pieces[4]()
        self.low = own[:half] + self.behind[half:] + ahead.astype(F32)
        self.high = own[half:] + self.ahead[:half] + behind.astype(F32)
        return (
            jnp.concatenate([self.low[rows + part:].astype(BF), self.high[:part].astype(BF)], axis=0),
            self.high[part:rows + part].astype(BF),
        )

    def second_b(self, ahead, behind):
        rows, part, down = self.rows, self.part, self.down
        self.ahead2, self.behind2 = ahead.astype(F32), behind.astype(F32)
        return (
            (self.low[rows:rows + part] + self.ahead2[down:]).astype(BF),
            (self.high[rows + part:] + self.behind2[:down]).astype(BF),
        )

    def result(self, ahead, behind):
        rows, part, down = self.rows, self.part, self.down
        return jnp.concatenate(
            [
                self.low[:part] + self.behind2[down:] + ahead.astype(F32),
                self.low[part:rows] + self.ahead2[:down] + behind.astype(F32),
            ],
            axis=0,
        )


def both_ways(pair, axis):
    return shift(pair[0], axis, N, 1), shift(pair[1], axis, N, 3)


def packed_both_ways(one, two, axis):
    size = one[0].shape[0]
    moved = both_ways([jnp.concatenate([a, b], axis=0) for a, b in zip(one, two)], axis)
    return [m[:size] for m in moved], [m[size:] for m in moved]


def local(
    siglip_features,
    convnext_features,
    siglip_projection,
    convnext_projection,
    newline_embed,
    key_value_weight,
    tile_rank,
    row_end,
    key_value_grad,
    newline_grad,
):
    blocks = N * N
    z, x = lax.axis_index("z"), lax.axis_index("x")
    ylo, core, yhi = lax.axis_index("ylo"), lax.axis_index("core"), lax.axis_index("yhi")
    my_rank = z * N + x
    member = (ylo * 2 + core) * 2 + yhi
    tiles = tile_rank.shape[0]
    per_device = tiles // blocks
    rows = siglip_features.shape[0]
    share = siglip_projection.shape[1]
    half = share // 2
    kv_rows = key_value_weight.shape[0] // blocks
    sig_rows = siglip_features.shape[1] // blocks
    conv_rows = convnext_features.shape[1] // blocks

    dest_rank = tile_rank.reshape(tiles)
    mine = lax.dynamic_slice_in_dim(dest_rank, my_rank * per_device, per_device)
    outgoing = slices_out(key_value_grad, member.reshape(1).astype(jnp.int32))
    received = lax.all_to_all(outgoing, DP, split_axis=0, concat_axis=0, tiled=True)

    projected = (
        jnp.dot(siglip_features, siglip_projection, preferred_element_type=F32)
        + jnp.dot(convnext_features, convnext_projection, preferred_element_type=F32)
    ).astype(BF)
    proj_values = projected.astype(F32)
    line_vector = newline_embed.astype(F32)
    squares = jnp.sum(proj_values * proj_values, axis=1).reshape(rows // 128, 128)
    line_square = jnp.broadcast_to(jnp.sum(line_vector * line_vector), (4, 128))
    statistic = all_sum(jnp.concatenate([squares, line_square], axis=0))
    inverse = lax.rsqrt(statistic[: rows // 128].reshape(rows) / D + epsilon)[:, None]
    line_normed = (line_vector * lax.rsqrt(statistic[rows // 128, 0] / D + epsilon)).astype(BF).astype(F32)

    step = jnp.arange(blocks, dtype=jnp.int32)
    outer, inner = step // N, step % N
    table1 = ((z + inner) % N) * N + (x + outer) % N
    table2 = ((z + outer) % N) * N + (x + inner) % N
    weight = block_order(key_value_weight.reshape(blocks, kv_rows, share), table1).reshape(
        blocks * kv_rows, share
    )

    onehot = (dest_rank[:, None] == jnp.arange(blocks, dtype=jnp.int32)[None, :]).astype(jnp.int32)
    grouped = onehot.reshape(blocks, per_device, blocks)
    before = jnp.cumsum(grouped, axis=1) - grouped
    slot_place = jnp.sum(before * grouped, axis=2).reshape(tiles)
    slot = (jnp.arange(tiles, dtype=jnp.int32) // per_device) * CAP + slot_place
    live = (dest_rank == my_rank) & (row_end == 1)
    mask = jnp.sum(
        ((slot[:, None] == jnp.arange(blocks * CAP, dtype=jnp.int32)[None, :]) & live[:, None]).astype(
            jnp.int32
        ),
        axis=0,
    )
    line_total = jnp.dot(mask.astype(BF)[None, :], newline_grad, preferred_element_type=F32)[0]
    line_blocks = line_total.reshape(blocks, kv_rows)
    line1 = line_blocks[table1].reshape(blocks * kv_rows)[:, None]
    line2 = line_blocks[table2].reshape(blocks * kv_rows)[:, None]

    received, weight, projected = lax.optimization_barrier((received, weight, projected))
    proj_values = projected.astype(F32)
    normed = (proj_values * inverse).astype(BF)
    own = pick_tiles(received.reshape(blocks * CAP, TT, received.shape[2]), mine).reshape(
        rows, received.shape[2]
    )
    own, siglip_features, convnext_features = lax.optimization_barrier(
        (own, siglip_features, convnext_features)
    )
    ring = [own] + [shift_y(own, s) for s in (1, 3, 2)]
    pieces = ring + [shift(piece, "core", 2, 1) for piece in ring]
    places = []
    y = yhi * 2 + ylo
    for side in (0, 1):
        for s in (0, 1, 3, 2):
            other = (y - s) % N
            places.append(((other % 2) * 2 + (core + side) % 2) * 2 + other // 2)
    features = jnp.concatenate(
        [
            siglip_features.T.reshape(blocks, sig_rows, rows),
            convnext_features.T.reshape(blocks, conv_rows, rows),
        ],
        axis=1,
    )
    x_rows = sig_rows + conv_rows
    features1, features2 = cut_orders(features, jnp.concatenate([table1, table2]))
    grads, grads1, grads2 = assemble(pieces, jnp.stack(places).astype(jnp.int32))

    left, right = slice(0, half), slice(half, share)

    def kv_pieces(cuts, line, columns):
        def piece(cut, start, stop):
            lines = line[start * kv_rows:stop * kv_rows]
            return lambda: (
                lax.dot_general(
                    cut, normed[:, columns], (((0,), (0,)), ((), ())), preferred_element_type=F32
                )
                + lines * line_normed[None, columns]
            )

        return [piece(cut, *where) for cut, where in zip(cuts, CUTS)]

    kv0 = Sums(kv_pieces(grads1, line1, left), kv_rows, kv_rows // 2)
    kv1 = Sums(kv_pieces(grads2, line2, right), kv_rows, kv_rows // 2)
    out0, out1 = kv0.first_a(), kv1.first_a()
    out0, out1, grads = lax.optimization_barrier((out0, out1, grads))
    in0, in1 = both_ways(out0, "x"), both_ways(out1, "z")

    grad_values = jnp.dot(grads, weight, preferred_element_type=F32).astype(BF).astype(F32)
    products = jnp.sum(grad_values * proj_values, axis=1).reshape(rows // 128, 128)
    members = 8
    products = jnp.sum(
        lax.all_to_all(
            jnp.broadcast_to(products[None], (members,) + products.shape),
            ("ylo", "core", "yhi"),
            split_axis=0,
            concat_axis=0,
            tiled=True,
        ),
        axis=0,
    )
    products = products.reshape(rows)[:, None]
    projected_grad = (
        inverse * grad_values - inverse**3 * proj_values * products / D
    ).astype(BF)
    out0, out1 = kv0.first_b(*in0), kv1.first_b(*in1)
    in0, in1 = both_ways(out0, "x"), both_ways(out1, "z")
    kv_out0, kv_out1 = kv0.second_a(*in0), kv1.second_a(*in1)

    def x_pieces(cuts, columns):
        return [
            lambda cut=cut: jnp.dot(cut, projected_grad[:, columns], preferred_element_type=F32)
            for cut in cuts
        ]

    part = (x_rows // 2 + 7) // 8 * 8
    x0 = Sums(x_pieces(features1, left), x_rows, part)
    x1 = Sums(x_pieces(features2, right), x_rows, part)
    in0, in1 = both_ways(x0.first_a(), "x"), both_ways(x1.first_a(), "z")
    in0, kv_in1 = packed_both_ways(x0.first_b(*in0), kv_out1, "x")
    in1, kv_in0 = packed_both_ways(x1.first_b(*in1), kv_out0, "z")
    in0, kv_in0 = packed_both_ways(x0.second_a(*in0), kv0.second_b(*kv_in0), "z")
    in1, kv_in1 = packed_both_ways(x1.second_a(*in1), kv1.second_b(*kv_in1), "x")
    kv_result = jnp.concatenate([kv0.result(*kv_in0), kv1.result(*kv_in1)], axis=1)
    in0, in1 = both_ways(x0.second_b(*in0), "z"), both_ways(x1.second_b(*in1), "x")
    x_result = jnp.concatenate([x0.result(*in0), x1.result(*in1)], axis=1)
    return x_result[:sig_rows], x_result[sig_rows:], kv_result


def solution(mesh):
    fine = Mesh(mesh.devices.reshape(2, 2, N, N, 2), ("ylo", "core", "z", "x", "yhi"))
    wide = ("ylo", "core", "yhi")
    in_specs = (
        P(DP, None),
        P(DP, None),
        P(None, wide),
        P(None, wide),
        P(wide),
        P(None, wide),
        P(),
        P(),
        P(DP, None),
        P(DP, None),
    )
    out_specs = (P(DP, wide), P(DP, wide), P(DP, wide))
    return jax.shard_map(local, mesh=fine, in_specs=in_specs, out_specs=out_specs, check_vma=False)
```

```python
import jax
import jax.numpy as jnp
from jax import lax
from jax.experimental import pallas as pl
from jax.experimental.pallas import tpu as pltpu
from jax.sharding import Mesh, PartitionSpec as P

D = 8192
epsilon = 1e-06
N = 4
TT = 32
CAP = 2
BF = jnp.bfloat16
F32 = jnp.float32
DP = ("z", "x")
Y = ("ylo", "yhi")


def shift(value, axis, size, step):
    return lax.ppermute(value, axis, [(i, (i + step) % size) for i in range(size)])


def shift_y(value, step):
    place = lambda y: (y % 2) * 2 + y // 2
    return lax.ppermute(value, Y, [(place(y), place((y + step) % N)) for y in range(N)])


EXTRA = 16
ANY = pl.ANY
HBM = pltpu.HBM
VMEM = pltpu.VMEM


def thirds(value):
    high = lax.reduce_precision(value, 8, 7)
    rest = value - high
    middle = lax.reduce_precision(rest, 8, 7)
    return high, middle, rest - middle


def extra_rows(rows):
    rows = jnp.concatenate(rows, axis=0)
    return jnp.pad(rows, ((0, EXTRA - rows.shape[0]), (0, 0))).astype(BF)


def order_blocks():
    z, x = lax.axis_index("z"), lax.axis_index("x")
    places = [(place // N, place % N) for place in range(N * N)]
    first = [((z + b) & 3) * N + ((x + a) & 3) for a, b in places]
    second = [((z + a) & 3) * N + ((x + b) & 3) for a, b in places]
    return first, second


def slices_out(key_value_grad, newline_grad):
    blocks = N * N
    rows = key_value_grad.shape[0] // blocks
    width = key_value_grad.shape[1] // blocks
    fold = newline_grad.shape[0] // 2

    def kernel(source, lines, out, sems):
        me = (lax.axis_index("ylo") * 2 + lax.axis_index("core")) * 2 + lax.axis_index("yhi")
        copies = []

        def move(origin, target):
            copy = pltpu.make_async_copy(origin, target, sems.at[len(copies)])
            copy.start()
            copies.append(copy)

        for dest in range(blocks):
            for part in range(2):
                place = 2 * me + part
                dx, dz = place >> 2, place & 3
                column = ((dest // N + dz) & 3) * N + ((dest % N + dx) & 3)
                move(
                    source.at[pl.ds(dest * rows, rows), pl.ds(pl.multiple_of(column * width, width), width)],
                    out.at[dest, pl.ds(0, rows), pl.ds(part * width, width)],
                )
                move(
                    lines.at[pl.ds(part * fold, fold), pl.ds(dest * width, width)],
                    out.at[dest, pl.ds(rows, fold), pl.ds(part * width, width)],
                )
        for copy in copies:
            copy.wait()

    return pl.pallas_call(
        kernel,
        out_shape=jax.ShapeDtypeStruct((blocks, rows + fold, 2 * width), key_value_grad.dtype),
        grid_spec=pltpu.PrefetchScalarGridSpec(
            num_scalar_prefetch=0,
            grid=(1,),
            in_specs=[pl.BlockSpec(memory_space=pl.ANY)] * 2,
            out_specs=pl.BlockSpec(memory_space=pltpu.VMEM),
            scratch_shapes=[pltpu.SemaphoreType.DMA((4 * blocks,))],
        ),
        name="slices_out",
    )(key_value_grad, newline_grad)


CUTS = ((6, 10), (10, 14), (4, 6), (14, 16), (0, 4))


def turn_features(siglip_features, convnext_features):
    rows = siglip_features.shape[0]
    blocks = N * N
    sizes = [siglip_features.shape[1] // blocks, convnext_features.shape[1] // blocks]
    size = sum(sizes)

    def kernel(siglip_ref, convnext_ref, *refs):
        count = 2 * len(CUTS)
        outs, staged, scratch, sems = refs[:count], refs[count:2 * count], refs[2 * count:-1], refs[-1]
        for source, target in zip((siglip_ref, convnext_ref), scratch):
            for i in range(source.shape[1] // 128):
                at = slice(i * 128, (i + 1) * 128)
                target[at] = source[:, at].T.astype(F32)
        first, _ = order_blocks()

        def store(order, place, value):
            for piece, (start, stop) in enumerate(CUTS):
                if start <= place < stop:
                    at = (place - start) * size
                    staged[order * len(CUTS) + piece][at:at + size] = value

        for place in range(blocks):
            value = jnp.concatenate(
                [
                    source[pl.ds(pl.multiple_of(first[place] * n, 8), n)]
                    for source, n in zip(scratch, sizes)
                ],
                axis=0,
            ).astype(BF)
            store(0, place, value)
            store(1, (place % N) * N + place // N, value)
        copies = [pltpu.make_async_copy(staged[i], outs[i], sems.at[i]) for i in range(count)]
        for copy in copies:
            copy.start()
        for copy in copies:
            copy.wait()

    shapes = [
        jax.ShapeDtypeStruct(((stop - start) * size, rows), siglip_features.dtype) for start, stop in CUTS
    ] * 2
    outs = pl.pallas_call(
        kernel,
        out_shape=[pltpu.HBM(shape.shape, shape.dtype) for shape in shapes],
        grid_spec=pltpu.PrefetchScalarGridSpec(
            num_scalar_prefetch=0,
            grid=(1,),
            in_specs=[
                pl.BlockSpec(siglip_features.shape, lambda i: (0, 0)),
                pl.BlockSpec(convnext_features.shape, lambda i: (0, 0)),
            ],
            out_specs=[pl.BlockSpec(memory_space=pltpu.HBM)] * len(shapes),
            scratch_shapes=[pltpu.VMEM(shape.shape, shape.dtype) for shape in shapes]
            + [
                pltpu.VMEM((siglip_features.shape[1], rows), F32),
                pltpu.VMEM((convnext_features.shape[1], rows), F32),
                pltpu.SemaphoreType.DMA((len(shapes),)),
            ],
        ),
        compiler_params=pltpu.CompilerParams(vmem_limit_bytes=32 * 1024 * 1024),
        name="turn_features",
    )(siglip_features, convnext_features)
    return outs[:len(CUTS)], outs[len(CUTS):]


def pick_tiles(received, dests, extra):
    tiles = dests.shape[0]
    width = received.shape[2]
    rows = tiles * TT

    def kernel(dest_ref, source, extra_ref, out, sems):
        names = [dest_ref[j] for j in range(tiles)]
        copies = []
        for j in range(tiles):
            before = jnp.int32(0)
            for i in range(j):
                before = before + (names[i] == names[j]).astype(jnp.int32)
            copy = pltpu.make_async_copy(
                source.at[names[j], pl.ds(pl.multiple_of(before * TT, TT), TT)],
                out.at[pl.ds(j * TT, TT)],
                sems.at[j],
            )
            copy.start()
            copies.append(copy)
        out[rows:] = extra_ref[...]
        for copy in copies:
            copy.wait()

    return pl.pallas_call(
        kernel,
        out_shape=jax.ShapeDtypeStruct((rows + EXTRA, width), received.dtype),
        grid_spec=pltpu.PrefetchScalarGridSpec(
            num_scalar_prefetch=1,
            grid=(1,),
            in_specs=[
                pl.BlockSpec(memory_space=pltpu.HBM),
                pl.BlockSpec((EXTRA, width), lambda i, t: (0, 0)),
            ],
            out_specs=pl.BlockSpec((rows + EXTRA, width), lambda i, t: (0, 0)),
            scratch_shapes=[pltpu.SemaphoreType.DMA((tiles,))],
        ),
        name="pick_tiles",
    )(dests, received, extra)


def step(kernel, name, ins, outs, scratch, copies, limit=24):
    return pl.pallas_call(
        kernel,
        out_shape=[space(shape.shape, shape.dtype) for shape, space in outs],
        grid_spec=pltpu.PrefetchScalarGridSpec(
            num_scalar_prefetch=0,
            grid=(1,),
            in_specs=[pl.BlockSpec(memory_space=space) for _, space in ins],
            out_specs=[pl.BlockSpec(memory_space=space) for _, space in outs],
            scratch_shapes=list(scratch) + [pltpu.SemaphoreType.DMA((copies,))],
        ),
        compiler_params=pltpu.CompilerParams(vmem_limit_bytes=limit * 1024 * 1024),
        name=name,
    )(
        *[array if space is ANY else pltpu.with_memory_space_constraint(array, space) for array, space in ins],
    )


class Copies:
    def __init__(self, sems):
        self.sems, self.count = sems, 0

    def start(self, source, target):
        copy = pltpu.make_async_copy(source, target, self.sems.at[self.count])
        self.count += 1
        copy.start()
        return copy


def down(row):
    return jnp.broadcast_to(row, (128, row.shape[1])).T


CHUNK = 256


def tile_step(pieces, projected, key_value_weight, newline_embed):
    wide = pieces[0].shape[1]
    rows = pieces[0].shape[0] - EXTRA
    width = wide // 2
    count = len(pieces)
    blocks = 2 * count
    share = projected.shape[1]
    deep = rows // wide
    half = share // 2
    dtype = pieces[0].dtype

    def kernel(*refs):
        piece_refs = refs[:count]
        proj_hbm, weight_hbm, embed_ref = refs[count:count + 3]
        first_hbm, second_hbm, grad_hbm, normed_hbm = refs[count + 3:count + 7]
        sends, (products_ref, inverse_ref, line_ref) = refs[count + 7:count + 11], refs[count + 11:count + 14]
        sources, proj_ref, weight_ref, first, second, grad_ref, normed_ref, staged, whole, sems = refs[
            count + 14:
        ]
        copies = Copies(sems)
        arriving = [copies.start(piece_refs[p], sources.at[p]) for p in range(count)]
        waits = [copies.start(proj_hbm, proj_ref), copies.start(weight_hbm, weight_ref)]
        z, x, core = lax.axis_index("z"), lax.axis_index("x"), lax.axis_index("core")
        y = lax.axis_index("yhi") * 2 + lax.axis_index("ylo")
        extra = jnp.zeros((EXTRA, wide), F32)
        for p, (side, steps) in enumerate([(side, steps) for side in (0, 1) for steps in (0, 1, 3, 2)]):
            arriving[p].wait()
            extra = extra + sources[p, rows:].astype(F32)
            other = (y - steps) & 3
            member = ((other & 1) * 2 + ((core + side) & 1)) * 2 + (other >> 1)
            for part in range(2):
                place = 2 * member + part
                turn = (place & 3) * N + (place >> 2)
                block = ((z + (place & 3)) & 3) * N + ((x + (place >> 2)) & 3)
                value = sources[p, :rows, part * width:(part + 1) * width]
                whole[:, pl.ds(pl.multiple_of(block * width, width), width)] = value
                flipped = value.T
                first[place] = flipped
                second[turn] = flipped
        leaving = [copies.start(first, first_hbm), copies.start(second, second_hbm)]
        for i in range(deep):
            squares = extra[i:i + 1] + extra[deep + i:deep + i + 1] + extra[2 * deep + i:2 * deep + i + 1]
            inverse_ref[i * wide:(i + 1) * wide] = lax.rsqrt(down(squares) / D + epsilon)
        line = jnp.sum(
            jnp.sum(extra[3 * deep:3 * deep + 3], axis=0, keepdims=True), axis=1, keepdims=True
        )
        line = embed_ref[...].astype(F32) * lax.rsqrt(line / D + epsilon)
        line_ref[...] = line.astype(BF).astype(F32)
        waits[0].wait()
        for i in range(share // 128):
            at = slice(i * 128, (i + 1) * 128)
            normed_ref[:, at] = (proj_ref[:, at].astype(F32) * inverse_ref[...]).astype(BF)
        leaving.append(copies.start(normed_ref, normed_hbm))
        for i in range(4):
            start, stop = CUTS[i % 2]
            left = (first, second)[i // 2][start:stop].reshape(N * width, rows)
            right = normed_ref[:, (i // 2) * half:(i // 2 + 1) * half]
            staged[i] = jnp.dot(left, right, preferred_element_type=F32).astype(BF)
            leaving.append(copies.start(staged.at[i], sends[i]))
        waits[1].wait()
        products = jnp.zeros((rows, 1), F32)
        for i in range(share // CHUNK):
            at = slice(i * CHUNK, (i + 1) * CHUNK)
            grad = jnp.dot(whole[...], weight_ref[:, at], preferred_element_type=F32).astype(BF)
            grad_ref[:, at] = grad
            leaving.append(copies.start(grad_ref.at[:, at], grad_hbm.at[:, at]))
            products = products + jnp.sum(
                grad.astype(F32) * proj_ref[:, at].astype(F32), axis=1, keepdims=True
            )
        products = jnp.broadcast_to(products, (rows, 128)).T
        products = jnp.concatenate(
            [products[:1, i * 128:(i + 1) * 128] for i in range(rows // 128)]
            + [jnp.zeros((8 - rows // 128, 128), F32)],
            axis=0,
        )
        products_ref[...] = jnp.broadcast_to(products[None], products_ref.shape)
        for copy in leaving:
            copy.wait()

    turned = jax.ShapeDtypeStruct((blocks, width, rows), dtype)
    grad = jax.ShapeDtypeStruct((rows, share), BF)
    outs = step(
        kernel,
        "tile_step",
        [(piece, ANY) for piece in pieces]
        + [(projected, HBM), (key_value_weight, HBM), (newline_embed, VMEM)],
        [
            (turned, HBM),
            (turned, HBM),
            (grad, HBM),
            (grad, HBM),
        ]
        + [(jax.ShapeDtypeStruct((N * width, half), BF), HBM)] * 4
        + [
            (jax.ShapeDtypeStruct((count, 8, 128), F32), VMEM),
            (jax.ShapeDtypeStruct((rows, 128), F32), VMEM),
            (jax.ShapeDtypeStruct((1, share), F32), VMEM),
        ],
        [
            VMEM((count,) + pieces[0].shape, dtype),
            VMEM(projected.shape, BF),
            VMEM(key_value_weight.shape, BF),
            VMEM(turned.shape, dtype),
            VMEM(turned.shape, dtype),
            VMEM(grad.shape, BF),
            VMEM(grad.shape, BF),
            VMEM((4, N * width, half), BF),
            VMEM((rows, wide * count), dtype),
        ],
        count + 9 + share // CHUNK,
    )
    return outs[:2], outs[2:4], outs[4:8], outs[8:]


def rest(name, sources, rhs):
    rows, share = rhs.shape
    half = share // 2

    def kernel(*refs):
        source_refs, rhs_hbm, outs = refs[:6], refs[6], refs[7:13]
        held, rhs_ref, staged, sems = refs[13:19], refs[19], refs[20:22], refs[22]
        copies = Copies(sems)
        arriving = [copies.start(source_refs[i], held[i]) for i in range(6)]
        copies.start(rhs_hbm, rhs_ref).wait()
        leaving = []
        for i in (2, 5, 0, 1, 3, 4):
            arriving[i].wait()
            right = rhs_ref[:, (i // 3) * half:(i // 3 + 1) * half]
            value = jnp.dot(held[i][...], right, preferred_element_type=F32)
            if i % 3 == 2:
                staged[i // 3][...] = value
                leaving.append(copies.start(staged[i // 3], outs[i]))
            else:
                outs[i][...] = value
        for copy in leaving:
            copy.wait()

    shapes = [jax.ShapeDtypeStruct((source.shape[0], half), F32) for source in sources]
    outs = step(
        kernel,
        name,
        [(source, HBM) for source in sources] + [(rhs, HBM)],
        [(shape, HBM if i % 3 == 2 else VMEM) for i, shape in enumerate(shapes)],
        [VMEM(source.shape, BF) for source in sources]
        + [VMEM(rhs.shape, BF)]
        + [VMEM(shapes[i].shape, F32) for i in (2, 5)],
        9,
        limit=14,
    )
    return outs[:3], outs[3:]


def kv_rest(turned, normed):
    blocks, width, rows = turned[0].shape
    half = normed.shape[1] // 2

    def kernel(first_hbm, second_hbm, normed_hbm, *refs):
        outs, (first_ref, second_ref, normed_ref), staged, sems = refs[:6], refs[6:9], refs[9:11], refs[11]
        copies = Copies(sems)
        arriving = [
            copies.start(source.at[pl.ds(start, stop - start)], target.at[pl.ds(start, stop - start)])
            for source, target in ((first_hbm, first_ref), (second_hbm, second_ref))
            for start, stop in CUTS[2:]
        ]
        copies.start(normed_hbm, normed_ref).wait()
        leaving = []
        for i in (2, 5, 0, 1, 3, 4):
            arriving[i].wait()
            start, stop = CUTS[2 + i % 3]
            left = (first_ref, second_ref)[i // 3][start:stop].reshape((stop - start) * width, rows)
            right = normed_ref[:, (i // 3) * half:(i // 3 + 1) * half]
            value = jnp.dot(left, right, preferred_element_type=F32)
            if i % 3 == 2:
                staged[i // 3][...] = value
                leaving.append(copies.start(staged[i // 3], outs[i]))
            else:
                outs[i][...] = value
        for copy in leaving:
            copy.wait()

    shapes = [jax.ShapeDtypeStruct(((stop - start) * width, half), F32) for start, stop in CUTS[2:]] * 2
    outs = step(
        kernel,
        "kv_rest",
        [(turned[0], HBM), (turned[1], HBM), (normed, HBM)],
        [(shape, HBM if i % 3 == 2 else VMEM) for i, shape in enumerate(shapes)],
        [VMEM(turned[0].shape, BF)] * 2 + [VMEM(normed.shape, BF)] + [VMEM(shapes[2].shape, F32)] * 2,
        9,
        limit=12,
    )
    return outs[:3], outs[3:]


def x_first(products, grad, projected, inverse, features1, features2):
    rows, share = grad.shape
    half = share // 2
    size = features1[0].shape[0]

    def kernel(products_ref, grad_hbm, proj_hbm, inverse_ref, *refs):
        features, out_hbm, sends = refs[:4], refs[4], refs[5:9]
        grad_ref, proj_ref, out, sources, staged, sems = refs[9:]
        copies = Copies(sems)
        ready = [copies.start(grad_hbm, grad_ref), copies.start(proj_hbm, proj_ref)]
        arriving = [copies.start(features[i], sources.at[i]) for i in range(4)]
        total = jnp.sum(products_ref[...], axis=0)
        total = jnp.concatenate([down(total[i:i + 1]) for i in range(rows // 128)], axis=0)
        inv = inverse_ref[...]
        scale = inv * inv * inv * total / D
        for copy in ready:
            copy.wait()
        for i in range(share // 128):
            at = slice(i * 128, (i + 1) * 128)
            out[:, at] = (
                inv * grad_ref[:, at].astype(F32) - scale * proj_ref[:, at].astype(F32)
            ).astype(BF)
        leaving = [copies.start(out, out_hbm)]
        for i in range(4):
            arriving[i].wait()
            right = out[:, (i // 2) * half:(i // 2 + 1) * half]
            staged[i] = jnp.dot(sources[i], right, preferred_element_type=F32).astype(BF)
            leaving.append(copies.start(staged.at[i], sends[i]))
        for copy in leaving:
            copy.wait()

    outs = step(
        kernel,
        "x_first",
        [(products, VMEM), (grad, HBM), (projected, HBM), (inverse, VMEM)]
        + [(cut, HBM) for cut in (features1[0], features1[1], features2[0], features2[1])],
        [(jax.ShapeDtypeStruct((rows, share), BF), HBM)]
        + [(jax.ShapeDtypeStruct((size, half), BF), HBM)] * 4,
        [
            VMEM(grad.shape, BF),
            VMEM(projected.shape, BF),
            VMEM(grad.shape, BF),
            VMEM((4,) + features1[0].shape, BF),
            VMEM((4, size, half), BF),
        ],
        11,
        limit=16,
    )
    return outs[0], outs[1:3], outs[3:5]


class Sums:
    def __init__(self, partials, rows, part):
        self.partials = partials
        self.rows, self.part = rows, part
        self.half, self.down = 2 * rows, rows - part

    def first_b(self, ahead, behind):
        self.ahead, self.behind = ahead, behind
        return (
            (self.partials[0] + ahead[self.half:].astype(F32)).astype(BF),
            (self.partials[1] + behind[:self.half].astype(F32)).astype(BF),
        )

    def second_a(self, ahead, behind):
        half, rows, part = self.half, self.rows, self.part
        own = self.partials[2]
        self.low = own[:half] + self.behind[half:].astype(F32) + ahead.astype(F32)
        self.high = own[half:] + self.ahead[:half].astype(F32) + behind.astype(F32)
        return (
            jnp.concatenate([self.low[rows + part:].astype(BF), self.high[:part].astype(BF)], axis=0),
            self.high[part:rows + part].astype(BF),
        )

    def second_b(self, ahead, behind):
        rows, part, down = self.rows, self.part, self.down
        self.ahead2, self.behind2 = ahead, behind
        return (
            (self.low[rows:rows + part] + ahead[down:].astype(F32)).astype(BF),
            (self.high[rows + part:] + behind[:down].astype(F32)).astype(BF),
        )

    def result(self, ahead, behind):
        rows, part, down = self.rows, self.part, self.down
        return jnp.concatenate(
            [
                self.low[:part] + self.behind2[down:].astype(F32) + ahead.astype(F32),
                self.low[part:rows] + self.ahead2[:down].astype(F32) + behind.astype(F32),
            ],
            axis=0,
        )


def both_ways(pair, axis):
    return shift(pair[0], axis, N, 1), shift(pair[1], axis, N, 3)


def packed_both_ways(one, two, axis):
    moved = both_ways([jnp.concatenate([a, b], axis=0) for a, b in zip(one, two)], axis)
    return [m[:a.shape[0]] for m, a in zip(moved, one)], [m[a.shape[0]:] for m, a in zip(moved, one)]


def local(
    siglip_features,
    convnext_features,
    siglip_projection,
    convnext_projection,
    newline_embed,
    key_value_weight,
    tile_rank,
    row_end,
    key_value_grad,
    newline_grad,
):
    blocks = N * N
    z, x = lax.axis_index("z"), lax.axis_index("x")
    my_rank = z * N + x
    tiles = tile_rank.shape[0]
    per_device = tiles // blocks
    rows = siglip_features.shape[0]
    share = siglip_projection.shape[1]
    half = share // 2
    kv_rows = key_value_weight.shape[0] // blocks
    sig_rows = siglip_features.shape[1] // blocks
    conv_rows = convnext_features.shape[1] // blocks

    dest_rank = tile_rank.reshape(tiles)
    mine = lax.dynamic_slice_in_dim(dest_rank, my_rank * per_device, per_device)
    outgoing = slices_out(key_value_grad, newline_grad)
    received = lax.all_to_all(outgoing, DP, split_axis=0, concat_axis=0, tiled=True)

    projected = (
        jnp.dot(siglip_features, siglip_projection, preferred_element_type=F32)
        + jnp.dot(convnext_features, convnext_projection, preferred_element_type=F32)
    ).astype(BF)
    proj_values = projected.astype(F32)
    line_vector = newline_embed.astype(F32)
    wide = received.shape[2]
    deep = rows // wide
    squares = jnp.sum(proj_values * proj_values, axis=1).reshape(deep, wide)
    line_squares = jnp.sum((line_vector * line_vector).reshape(share // wide, wide), axis=0)[None]
    statistics = extra_rows(thirds(squares) + thirds(line_squares))

    features1, features2 = turn_features(siglip_features, convnext_features)
    x_rows = sig_rows + conv_rows
    received, statistics, features1, features2 = lax.optimization_barrier(
        (received, statistics, features1, features2)
    )
    own = pick_tiles(received, mine, statistics)
    own, received, dest_rank, row_end = lax.optimization_barrier((own, received, dest_rank, row_end))
    ring = [own] + [shift_y(own, s) for s in (1, 3, 2)]
    pieces = ring + [shift(piece, "core", 2, 1) for piece in ring]

    onehot = (dest_rank[:, None] == jnp.arange(blocks, dtype=jnp.int32)[None, :]).astype(jnp.int32)
    grouped = onehot.reshape(blocks, per_device, blocks)
    before = jnp.cumsum(grouped, axis=1) - grouped
    slot_place = jnp.sum(before * grouped, axis=2).reshape(tiles)
    slot = (jnp.arange(tiles, dtype=jnp.int32) // per_device) * CAP + slot_place
    slot_index = dest_rank * (blocks * CAP) + slot
    mask = jnp.sum(
        (
            (slot_index[:, None] == jnp.arange(blocks * blocks * CAP, dtype=jnp.int32)[None, :])
            & (row_end[:, None] == 1)
        ).astype(F32),
        axis=0,
    ).astype(BF)
    mask = mask.reshape(blocks, 2, blocks)
    line_rows = received[:, CAP * TT:]
    line_total = sum(
        jnp.dot(
            mask[:, part].reshape(1, blocks * blocks),
            line_rows[:, :, part * kv_rows:(part + 1) * kv_rows].reshape(blocks * blocks, kv_rows),
            preferred_element_type=F32,
        )
        for part in range(2)
    )
    line_total = jnp.broadcast_to(line_total, (kv_rows, kv_rows)).T

    turned, (normed_grad, normed), kv_sends, (products, inverse, line_normed) = tile_step(
        pieces, projected, key_value_weight, newline_embed.reshape(1, share)
    )
    products = lax.all_to_all(products, ("ylo", "core", "yhi"), split_axis=0, concat_axis=0, tiled=True)

    in0, in1 = both_ways(kv_sends[:2], "x"), both_ways(kv_sends[2:], "z")
    kv_parts0, kv_parts1 = kv_rest(turned, normed)
    kv0 = Sums(kv_parts0, kv_rows, kv_rows // 2)
    kv1 = Sums(kv_parts1, kv_rows, kv_rows // 2)
    out0, out1 = kv0.first_b(*in0), kv1.first_b(*in1)

    projected_grad, x_send0, x_send1 = x_first(
        products, normed_grad, projected, inverse, features1, features2
    )
    x_in0, x_in1 = both_ways(x_send0, "x"), both_ways(x_send1, "z")
    out0, out1, projected_grad = lax.optimization_barrier((out0, out1, projected_grad))
    in0, in1 = both_ways(out0, "x"), both_ways(out1, "z")
    kv_out0, kv_out1 = kv0.second_a(*in0), kv1.second_a(*in1)
    in0, in1 = x_in0, x_in1
    x_parts0, x_parts1 = rest("x_rest", list(features1[2:]) + list(features2[2:]), projected_grad)
    part = (x_rows // 2 + 7) // 8 * 8
    x0 = Sums(x_parts0, x_rows, part)
    x1 = Sums(x_parts1, x_rows, part)
    in0, in1 = both_ways(x0.first_b(*in0), "x"), both_ways(x1.first_b(*in1), "z")
    in0, kv_in0 = packed_both_ways(x0.second_a(*in0), kv_out0, "z")
    in1, kv_in1 = packed_both_ways(x1.second_a(*in1), kv_out1, "x")
    in0, kv_in0 = packed_both_ways(x0.second_b(*in0), kv0.second_b(*kv_in0), "z")
    in1, kv_in1 = packed_both_ways(x1.second_b(*in1), kv1.second_b(*kv_in1), "x")
    kv_result = jnp.concatenate([kv0.result(*kv_in0), kv1.result(*kv_in1)], axis=1)
    kv_result = kv_result + line_total[:, :1] * line_normed
    x_result = jnp.concatenate([x0.result(*in0), x1.result(*in1)], axis=1)
    return x_result[:sig_rows], x_result[sig_rows:], kv_result


def solution(mesh):
    fine = Mesh(mesh.devices.reshape(2, 2, N, N, 2), ("ylo", "core", "z", "x", "yhi"))
    wide = ("ylo", "core", "yhi")
    in_specs = (
        P(DP, None),
        P(DP, None),
        P(None, wide),
        P(None, wide),
        P(wide),
        P(None, wide),
        P(),
        P(),
        P(DP, None),
        P(DP, None),
    )
    out_specs = (P(DP, wide), P(DP, wide), P(DP, wide))
    return jax.shard_map(local, mesh=fine, in_specs=in_specs, out_specs=out_specs, check_vma=False)
```

```python
import jax
import jax.numpy as jnp
from jax import lax
from jax.experimental import pallas as pl
from jax.experimental.pallas import tpu as pltpu
from jax.sharding import Mesh, PartitionSpec as P

D = 8192
epsilon = 1e-06
N = 4
TT = 32
CAP = 2
BF = jnp.bfloat16
F32 = jnp.float32
DP = ("z", "x")
Y = ("ylo", "yhi")


def shift(value, axis, size, step):
    return lax.ppermute(value, axis, [(i, (i + step) % size) for i in range(size)])


def shift_y(value, step):
    place = lambda y: (y % 2) * 2 + y // 2
    return lax.ppermute(value, Y, [(place(y), place((y + step) % N)) for y in range(N)])


EXTRA = 16
ANY = pl.ANY
HBM = pltpu.HBM
VMEM = pltpu.VMEM


def thirds(value):
    high = lax.reduce_precision(value, 8, 7)
    rest = value - high
    middle = lax.reduce_precision(rest, 8, 7)
    return high, middle, rest - middle


def extra_rows(rows):
    rows = jnp.concatenate(rows, axis=0)
    return jnp.pad(rows, ((0, EXTRA - rows.shape[0]), (0, 0))).astype(BF)


def order_blocks():
    z, x = lax.axis_index("z"), lax.axis_index("x")
    places = [(place // N, place % N) for place in range(N * N)]
    first = [((z + b) & 3) * N + ((x + a) & 3) for a, b in places]
    second = [((z + a) & 3) * N + ((x + b) & 3) for a, b in places]
    return first, second


def slices_out(key_value_grad, newline_grad):
    blocks = N * N
    rows = key_value_grad.shape[0] // blocks
    width = key_value_grad.shape[1] // blocks
    fold = newline_grad.shape[0] // 2

    def kernel(source, lines, out, sems):
        me = (lax.axis_index("ylo") * 2 + lax.axis_index("core")) * 2 + lax.axis_index("yhi")
        copies = []

        def move(origin, target):
            copy = pltpu.make_async_copy(origin, target, sems.at[len(copies)])
            copy.start()
            copies.append(copy)

        for dest in range(blocks):
            for part in range(2):
                place = 2 * me + part
                dx, dz = place >> 2, place & 3
                column = ((dest // N + dz) & 3) * N + ((dest % N + dx) & 3)
                move(
                    source.at[pl.ds(dest * rows, rows), pl.ds(pl.multiple_of(column * width, width), width)],
                    out.at[dest, pl.ds(0, rows), pl.ds(part * width, width)],
                )
                move(
                    lines.at[pl.ds(part * fold, fold), pl.ds(dest * width, width)],
                    out.at[dest, pl.ds(rows, fold), pl.ds(part * width, width)],
                )
        for copy in copies:
            copy.wait()

    return pl.pallas_call(
        kernel,
        out_shape=jax.ShapeDtypeStruct((blocks, rows + fold, 2 * width), key_value_grad.dtype),
        grid_spec=pltpu.PrefetchScalarGridSpec(
            num_scalar_prefetch=0,
            grid=(1,),
            in_specs=[pl.BlockSpec(memory_space=pl.ANY)] * 2,
            out_specs=pl.BlockSpec(memory_space=pltpu.VMEM),
            scratch_shapes=[pltpu.SemaphoreType.DMA((4 * blocks,))],
        ),
        name="slices_out",
    )(key_value_grad, newline_grad)


CUTS = ((6, 10), (10, 14), (4, 6), (14, 16), (0, 4))


def turn_features(siglip_features, convnext_features):
    rows = siglip_features.shape[0]
    blocks = N * N
    sizes = [siglip_features.shape[1] // blocks, convnext_features.shape[1] // blocks]
    size = sum(sizes)

    def kernel(siglip_ref, convnext_ref, *refs):
        count = 2 * len(CUTS)
        outs, staged, scratch, sems = refs[:count], refs[count:2 * count], refs[2 * count:-1], refs[-1]
        for source, target in zip((siglip_ref, convnext_ref), scratch):
            for i in range(source.shape[1] // 128):
                at = slice(i * 128, (i + 1) * 128)
                target[at] = source[:, at].T.astype(F32)
        first, _ = order_blocks()

        def store(order, place, value):
            for piece, (start, stop) in enumerate(CUTS):
                if start <= place < stop:
                    at = (place - start) * size
                    staged[order * len(CUTS) + piece][at:at + size] = value

        for place in range(blocks):
            value = jnp.concatenate(
                [
                    source[pl.ds(pl.multiple_of(first[place] * n, 8), n)]
                    for source, n in zip(scratch, sizes)
                ],
                axis=0,
            ).astype(BF)
            store(0, place, value)
            store(1, (place % N) * N + place // N, value)
        copies = [pltpu.make_async_copy(staged[i], outs[i], sems.at[i]) for i in range(count)]
        for copy in copies:
            copy.start()
        for copy in copies:
            copy.wait()

    shapes = [
        jax.ShapeDtypeStruct(((stop - start) * size, rows), siglip_features.dtype) for start, stop in CUTS
    ] * 2
    outs = pl.pallas_call(
        kernel,
        out_shape=[pltpu.HBM(shape.shape, shape.dtype) for shape in shapes],
        grid_spec=pltpu.PrefetchScalarGridSpec(
            num_scalar_prefetch=0,
            grid=(1,),
            in_specs=[
                pl.BlockSpec(siglip_features.shape, lambda i: (0, 0)),
                pl.BlockSpec(convnext_features.shape, lambda i: (0, 0)),
            ],
            out_specs=[pl.BlockSpec(memory_space=pltpu.HBM)] * len(shapes),
            scratch_shapes=[pltpu.VMEM(shape.shape, shape.dtype) for shape in shapes]
            + [
                pltpu.VMEM((siglip_features.shape[1], rows), F32),
                pltpu.VMEM((convnext_features.shape[1], rows), F32),
                pltpu.SemaphoreType.DMA((len(shapes),)),
            ],
        ),
        compiler_params=pltpu.CompilerParams(vmem_limit_bytes=32 * 1024 * 1024),
        name="turn_features",
    )(siglip_features, convnext_features)
    return outs[:len(CUTS)], outs[len(CUTS):]


def pick_tiles(received, dests, extra):
    tiles = dests.shape[0]
    width = received.shape[2]
    rows = tiles * TT

    def kernel(dest_ref, source, extra_ref, out, sems):
        names = [dest_ref[j] for j in range(tiles)]
        copies = []
        for j in range(tiles):
            before = jnp.int32(0)
            for i in range(j):
                before = before + (names[i] == names[j]).astype(jnp.int32)
            copy = pltpu.make_async_copy(
                source.at[names[j], pl.ds(pl.multiple_of(before * TT, TT), TT)],
                out.at[pl.ds(j * TT, TT)],
                sems.at[j],
            )
            copy.start()
            copies.append(copy)
        out[rows:] = extra_ref[...]
        for copy in copies:
            copy.wait()

    return pl.pallas_call(
        kernel,
        out_shape=jax.ShapeDtypeStruct((rows + EXTRA, width), received.dtype),
        grid_spec=pltpu.PrefetchScalarGridSpec(
            num_scalar_prefetch=1,
            grid=(1,),
            in_specs=[
                pl.BlockSpec(memory_space=pltpu.HBM),
                pl.BlockSpec((EXTRA, width), lambda i, t: (0, 0)),
            ],
            out_specs=pl.BlockSpec((rows + EXTRA, width), lambda i, t: (0, 0)),
            scratch_shapes=[pltpu.SemaphoreType.DMA((tiles,))],
        ),
        name="pick_tiles",
    )(dests, received, extra)


def step(kernel, name, ins, outs, scratch, copies, limit=24):
    return pl.pallas_call(
        kernel,
        out_shape=[space(shape.shape, shape.dtype) for shape, space in outs],
        grid_spec=pltpu.PrefetchScalarGridSpec(
            num_scalar_prefetch=0,
            grid=(1,),
            in_specs=[pl.BlockSpec(memory_space=space) for _, space in ins],
            out_specs=[pl.BlockSpec(memory_space=space) for _, space in outs],
            scratch_shapes=list(scratch) + [pltpu.SemaphoreType.DMA((copies,))],
        ),
        compiler_params=pltpu.CompilerParams(vmem_limit_bytes=limit * 1024 * 1024),
        name=name,
    )(
        *[array if space is ANY else pltpu.with_memory_space_constraint(array, space) for array, space in ins],
    )


class Copies:
    def __init__(self, sems):
        self.sems, self.count = sems, 0

    def start(self, source, target):
        copy = pltpu.make_async_copy(source, target, self.sems.at[self.count])
        self.count += 1
        copy.start()
        return copy


def down(row):
    return jnp.broadcast_to(row, (128, row.shape[1])).T


CHUNK = 256
FAR = (2, 1, 3)


def tile_step(pieces, projected, key_value_weight, newline_embed):
    wide = pieces[0].shape[1]
    rows = pieces[0].shape[0] - EXTRA
    width = wide // 2
    count = len(pieces)
    blocks = 2 * count
    share = projected.shape[1]
    deep = rows // wide
    half = share // 2
    dtype = pieces[0].dtype

    def kernel(*refs):
        piece_refs = refs[:count]
        proj_hbm, weight_hbm, embed_ref = refs[count:count + 3]
        kept, (grad_hbm, normed_hbm) = refs[count + 3:count + 9], refs[count + 9:count + 11]
        sends, (products_ref, inverse_ref, line_ref) = refs[count + 11:count + 15], refs[count + 15:count + 18]
        sources, proj_ref, weight_ref, first, second, grad_ref, normed_ref, staged, whole, sems = refs[
            count + 18:
        ]
        copies = Copies(sems)
        arriving = [copies.start(piece_refs[p], sources.at[p]) for p in range(count)]
        waits = [copies.start(proj_hbm, proj_ref), copies.start(weight_hbm, weight_ref)]
        z, x, core = lax.axis_index("z"), lax.axis_index("x"), lax.axis_index("core")
        y = lax.axis_index("yhi") * 2 + lax.axis_index("ylo")
        extra = jnp.zeros((EXTRA, wide), F32)
        for p, (side, steps) in enumerate([(side, steps) for side in (0, 1) for steps in (0, 1, 3, 2)]):
            arriving[p].wait()
            extra = extra + sources[p, rows:].astype(F32)
            other = (y - steps) & 3
            member = ((other & 1) * 2 + ((core + side) & 1)) * 2 + (other >> 1)
            for part in range(2):
                place = 2 * member + part
                turn = (place & 3) * N + (place >> 2)
                block = ((z + (place & 3)) & 3) * N + ((x + (place >> 2)) & 3)
                value = sources[p, :rows, part * width:(part + 1) * width]
                whole[:, pl.ds(pl.multiple_of(block * width, width), width)] = value
                flipped = value.T
                first[place] = flipped
                second[turn] = flipped
        leaving = [
            copies.start((first, second)[i // 3].at[pl.ds(start, stop - start)], kept[i])
            for i, (start, stop) in enumerate(CUTS[2:] * 2)
        ]
        for i in range(deep):
            squares = extra[i:i + 1] + extra[deep + i:deep + i + 1] + extra[2 * deep + i:2 * deep + i + 1]
            inverse_ref[i * wide:(i + 1) * wide] = lax.rsqrt(down(squares) / D + epsilon)
        line = jnp.sum(
            jnp.sum(extra[3 * deep:3 * deep + 3], axis=0, keepdims=True), axis=1, keepdims=True
        )
        line = embed_ref[...].astype(F32) * lax.rsqrt(line / D + epsilon)
        line_ref[...] = line.astype(BF).astype(F32)
        waits[0].wait()
        for i in range(share // 128):
            at = slice(i * 128, (i + 1) * 128)
            normed_ref[:, at] = (proj_ref[:, at].astype(F32) * inverse_ref[...]).astype(BF)
        leaving.append(copies.start(normed_ref, normed_hbm))
        for i in range(4):
            start, stop = CUTS[i % 2]
            left = (first, second)[i // 2][start:stop].reshape(N * width, rows)
            right = normed_ref[:, (i // 2) * half:(i // 2 + 1) * half]
            staged[i] = jnp.dot(left, right, preferred_element_type=F32).astype(BF)
            leaving.append(copies.start(staged.at[i], sends[i]))
        waits[1].wait()
        products = jnp.zeros((rows, 1), F32)
        for i in range(share // CHUNK):
            at = slice(i * CHUNK, (i + 1) * CHUNK)
            grad = jnp.dot(whole[...], weight_ref[:, at], preferred_element_type=F32).astype(BF)
            grad_ref[:, at] = grad
            leaving.append(copies.start(grad_ref.at[:, at], grad_hbm.at[:, at]))
            products = products + jnp.sum(
                grad.astype(F32) * proj_ref[:, at].astype(F32), axis=1, keepdims=True
            )
        products = jnp.broadcast_to(products, (rows, 128)).T
        products = jnp.concatenate(
            [products[:1, i * 128:(i + 1) * 128] for i in range(rows // 128)]
            + [jnp.zeros((8 - rows // 128, 128), F32)],
            axis=0,
        )
        products_ref[...] = jnp.broadcast_to(products[None], products_ref.shape)
        for copy in leaving:
            copy.wait()

    turned = jax.ShapeDtypeStruct((blocks, width, rows), dtype)
    grad = jax.ShapeDtypeStruct((rows, share), BF)
    outs = step(
        kernel,
        "tile_step",
        [(pieces[0], HBM)] + [(piece, ANY) for piece in pieces[1:]]
        + [(projected, HBM), (key_value_weight, HBM), (newline_embed, VMEM)],
        [(jax.ShapeDtypeStruct((stop - start, width, rows), dtype), HBM) for start, stop in CUTS[2:]] * 2
        + [
            (grad, HBM),
            (grad, HBM),
        ]
        + [(jax.ShapeDtypeStruct((N * width, half), BF), HBM)] * 4
        + [
            (jax.ShapeDtypeStruct((count, 8, 128), F32), VMEM),
            (jax.ShapeDtypeStruct((rows, 128), F32), VMEM),
            (jax.ShapeDtypeStruct((1, share), F32), VMEM),
        ],
        [
            VMEM((count,) + pieces[0].shape, dtype),
            VMEM(projected.shape, BF),
            VMEM(key_value_weight.shape, BF),
            VMEM(turned.shape, dtype),
            VMEM(turned.shape, dtype),
            VMEM(grad.shape, BF),
            VMEM(grad.shape, BF),
            VMEM((4, N * width, half), BF),
            VMEM((rows, wide * count), dtype),
        ],
        count + 13 + share // CHUNK,
    )
    return outs[:6], outs[6:8], outs[8:12], outs[12:]


def x_rest(features, projected_grad, turned, normed):
    rows, share = normed.shape
    half = share // 2
    lefts = list(features) + list(turned)
    arrays = lefts + [projected_grad, normed]
    count = len(lefts)
    tall = [left.size // rows for left in lefts]
    shapes = [jax.ShapeDtypeStruct((height, half), F32) for height in tall]

    def kernel(*refs):
        ins, outs = refs[:count + 2], refs[count + 2:2 * count + 2]
        held, sems = refs[2 * count + 2:-1], refs[-1]
        copies = Copies(sems)
        right_sides = [copies.start(ins[count + i], held[count + i]) for i in range(2)]
        arriving = [copies.start(ins[i], held[i]) for i in range(count)]
        for i in range(count):
            which = i // (count // 2)
            if i % (count // 2) == 0:
                right_sides[which].wait()
            arriving[i].wait()
            order = (i // 3) % 2
            right = held[count + which][:, order * half:(order + 1) * half]
            outs[i][...] = jnp.dot(
                held[i][...].reshape(tall[i], rows), right, preferred_element_type=F32
            )

    outs = step(
        kernel,
        "x_rest",
        [(array, HBM) for array in arrays],
        [(shape, VMEM) for shape in shapes],
        [VMEM(array.shape, BF) for array in arrays],
        count + 2,
        limit=16,
    )
    return outs[:3], outs[3:6], outs[6:9], outs[9:]


def x_first(products, grad, projected, inverse, features1, features2):
    rows, share = grad.shape
    half = share // 2
    size = features1[0].shape[0]

    def kernel(products_ref, grad_ref, proj_ref, inverse_ref, *refs):
        features, out_hbm, sends = refs[:4], refs[4], refs[5:9]
        out, staged, sems = refs[9:]
        copies = Copies(sems)
        total = jnp.sum(products_ref[...], axis=0)
        total = jnp.concatenate([down(total[i:i + 1]) for i in range(rows // 128)], axis=0)
        inv = inverse_ref[...]
        scale = inv * inv * inv * total / D
        for i in range(share // 128):
            at = slice(i * 128, (i + 1) * 128)
            out[:, at] = (
                inv * grad_ref[:, at].astype(F32) - scale * proj_ref[:, at].astype(F32)
            ).astype(BF)
        leaving = [copies.start(out, out_hbm)]
        for i in range(4):
            right = out[:, (i // 2) * half:(i // 2 + 1) * half]
            staged[i] = jnp.dot(features[i][...], right, preferred_element_type=F32).astype(BF)
            leaving.append(copies.start(staged.at[i], sends[i]))
        for copy in leaving:
            copy.wait()

    outs = step(
        kernel,
        "x_first",
        [(products, VMEM), (grad, VMEM), (projected, VMEM), (inverse, VMEM)]
        + [(cut, VMEM) for cut in (features1[0], features1[1], features2[0], features2[1])],
        [(jax.ShapeDtypeStruct((rows, share), BF), HBM)]
        + [(jax.ShapeDtypeStruct((size, half), BF), HBM)] * 4,
        [
            VMEM(grad.shape, BF),
            VMEM((4, size, half), BF),
        ],
        5,
        limit=12,
    )
    return outs[0], outs[1:3], outs[3:5]


def ring_sends(partials, ahead, behind):
    near, far, _ = partials
    half = near.shape[0]
    return (
        (near + ahead[half:].astype(F32)).astype(BF),
        (far + behind[:half].astype(F32)).astype(BF),
    )


def ring_blocks(partials, ahead, behind, ahead2, behind2):
    own = partials[2]
    half = own.shape[0] // 2
    low = own[:half] + behind[half:].astype(F32) + ahead2.astype(F32)
    high = own[half:] + ahead[:half].astype(F32) + behind2.astype(F32)
    size = half // 2
    return low[:size], low[size:], high[:size], high[size:]


def straight(blocks, axis):
    arrived = [shift(blocks[d].astype(BF), axis, N, d).astype(F32) for d in FAR]
    return blocks[0] + arrived[0] + arrived[1] + arrived[2]


def local(
    siglip_features,
    convnext_features,
    siglip_projection,
    convnext_projection,
    newline_embed,
    key_value_weight,
    tile_rank,
    row_end,
    key_value_grad,
    newline_grad,
):
    blocks = N * N
    z, x = lax.axis_index("z"), lax.axis_index("x")
    my_rank = z * N + x
    tiles = tile_rank.shape[0]
    per_device = tiles // blocks
    rows = siglip_features.shape[0]
    share = siglip_projection.shape[1]
    half = share // 2
    kv_rows = key_value_weight.shape[0] // blocks
    sig_rows = siglip_features.shape[1] // blocks
    conv_rows = convnext_features.shape[1] // blocks

    dest_rank = tile_rank.reshape(tiles)
    mine = lax.dynamic_slice_in_dim(dest_rank, my_rank * per_device, per_device)
    outgoing = slices_out(key_value_grad, newline_grad)
    received = lax.all_to_all(outgoing, DP, split_axis=0, concat_axis=0, tiled=True)

    projected = (
        jnp.dot(siglip_features, siglip_projection, preferred_element_type=F32)
        + jnp.dot(convnext_features, convnext_projection, preferred_element_type=F32)
    ).astype(BF)
    proj_values = projected.astype(F32)
    line_vector = newline_embed.astype(F32)
    wide = received.shape[2]
    deep = rows // wide
    squares = jnp.sum(proj_values * proj_values, axis=1).reshape(deep, wide)
    line_squares = jnp.sum((line_vector * line_vector).reshape(share // wide, wide), axis=0)[None]
    statistics = extra_rows(thirds(squares) + thirds(line_squares))

    features1, features2 = turn_features(siglip_features, convnext_features)
    x_rows = sig_rows + conv_rows
    received, statistics, features1, features2 = lax.optimization_barrier(
        (received, statistics, features1, features2)
    )
    own = pick_tiles(received, mine, statistics)
    own, received, dest_rank, row_end = lax.optimization_barrier((own, received, dest_rank, row_end))
    ring = [own] + [shift_y(own, s) for s in (1, 3, 2)]
    pieces = ring + [shift(piece, "core", 2, 1) for piece in ring]

    onehot = (dest_rank[:, None] == jnp.arange(blocks, dtype=jnp.int32)[None, :]).astype(jnp.int32)
    grouped = onehot.reshape(blocks, per_device, blocks)
    before = jnp.cumsum(grouped, axis=1) - grouped
    slot_place = jnp.sum(before * grouped, axis=2).reshape(tiles)
    slot = (jnp.arange(tiles, dtype=jnp.int32) // per_device) * CAP + slot_place
    slot_index = dest_rank * (blocks * CAP) + slot
    mask = jnp.sum(
        (
            (slot_index[:, None] == jnp.arange(blocks * blocks * CAP, dtype=jnp.int32)[None, :])
            & (row_end[:, None] == 1)
        ).astype(F32),
        axis=0,
    ).astype(BF)
    mask = mask.reshape(blocks, 2, blocks)
    line_rows = received[:, CAP * TT:]
    line_total = sum(
        jnp.dot(
            mask[:, part].reshape(1, blocks * blocks),
            line_rows[:, :, part * kv_rows:(part + 1) * kv_rows].reshape(blocks * blocks, kv_rows),
            preferred_element_type=F32,
        )
        for part in range(2)
    )
    line_total = jnp.broadcast_to(line_total, (kv_rows, kv_rows)).T

    newline_embed, line_total = lax.optimization_barrier((newline_embed, line_total))
    turned, (normed_grad, normed), kv_sends, (products, inverse, line_normed) = tile_step(
        pieces, projected, key_value_weight, newline_embed.reshape(1, share)
    )
    products = lax.all_to_all(products, ("ylo", "core", "yhi"), split_axis=0, concat_axis=0, tiled=True)

    def both_ways(pair, axis):
        return shift(pair[0], axis, N, 1), shift(pair[1], axis, N, 3)

    kv_in = [both_ways(kv_sends[:2], "x"), both_ways(kv_sends[2:], "z")]
    projected_grad, x_send0, x_send1 = x_first(
        products, normed_grad, projected, inverse, features1, features2
    )
    x_in = [both_ways(x_send0, "x"), both_ways(x_send1, "z")]
    kv_in, projected_grad = lax.optimization_barrier((kv_in, projected_grad))
    parts = x_rest(list(features1[2:]) + list(features2[2:]), projected_grad, turned, normed)
    results = []
    for i, (first, second) in enumerate((("x", "z"), ("z", "x"))):
        x_parts, kv_parts = parts[i], parts[2 + i]
        sends = [
            jnp.concatenate(pair, axis=0)
            for pair in zip(ring_sends(x_parts, *x_in[i]), ring_sends(kv_parts, *kv_in[i]))
        ]
        ahead, behind = both_ways(sends, first)
        size = x_parts[0].shape[0]
        x_blocks = ring_blocks(x_parts, *x_in[i], ahead[:size], behind[:size])
        kv_blocks = ring_blocks(kv_parts, *kv_in[i], ahead[size:], behind[size:])
        results.append(
            straight([jnp.concatenate(pair, axis=0) for pair in zip(x_blocks, kv_blocks)], second)
        )
    result = jnp.concatenate(results, axis=1)
    x_result, kv_result = result[:x_rows], result[x_rows:]
    kv_result = kv_result + line_total[:, :1] * line_normed
    return x_result[:sig_rows], x_result[sig_rows:], kv_result


def solution(mesh):
    fine = Mesh(mesh.devices.reshape(2, 2, N, N, 2), ("ylo", "core", "z", "x", "yhi"))
    wide = ("ylo", "core", "yhi")
    in_specs = (
        P(DP, None),
        P(DP, None),
        P(None, wide),
        P(None, wide),
        P(wide),
        P(None, wide),
        P(),
        P(),
        P(DP, None),
        P(DP, None),
    )
    out_specs = (P(DP, wide), P(DP, wide), P(DP, wide))
    return jax.shard_map(local, mesh=fine, in_specs=in_specs, out_specs=out_specs, check_vma=False)
```

```python
import jax
import jax.numpy as jnp
from jax import lax
from jax.experimental import pallas as pl
from jax.experimental.pallas import tpu as pltpu
from jax.sharding import Mesh, PartitionSpec as P

D = 8192
epsilon = 1e-06
N = 4
TT = 32
CAP = 2
BF = jnp.bfloat16
F32 = jnp.float32
DP = ("z", "x")
Y = ("ylo", "yhi")


def shift(value, axis, size, step):
    return lax.ppermute(value, axis, [(i, (i + step) % size) for i in range(size)])


def shift_y(value, step):
    place = lambda y: (y % 2) * 2 + y // 2
    return lax.ppermute(value, Y, [(place(y), place((y + step) % N)) for y in range(N)])


EXTRA = 16
ANY = pl.ANY
HBM = pltpu.HBM
VMEM = pltpu.VMEM


def thirds(value):
    high = lax.reduce_precision(value, 8, 7)
    rest = value - high
    middle = lax.reduce_precision(rest, 8, 7)
    return high, middle, rest - middle


def extra_rows(rows):
    rows = jnp.concatenate(rows, axis=0)
    return jnp.pad(rows, ((0, EXTRA - rows.shape[0]), (0, 0))).astype(BF)


def order_blocks():
    z, x = lax.axis_index("z"), lax.axis_index("x")
    places = [(place // N, place % N) for place in range(N * N)]
    first = [((z + b) & 3) * N + ((x + a) & 3) for a, b in places]
    second = [((z + a) & 3) * N + ((x + b) & 3) for a, b in places]
    return first, second


def slices_out(key_value_grad, newline_grad):
    blocks = N * N
    rows = key_value_grad.shape[0] // blocks
    width = key_value_grad.shape[1] // blocks
    fold = newline_grad.shape[0] // 2

    def kernel(source, lines, out, sems):
        me = (lax.axis_index("ylo") * 2 + lax.axis_index("core")) * 2 + lax.axis_index("yhi")
        copies = []

        def move(origin, target):
            copy = pltpu.make_async_copy(origin, target, sems.at[len(copies)])
            copy.start()
            copies.append(copy)

        for dest in range(blocks):
            for part in range(2):
                place = 2 * me + part
                dx, dz = place >> 2, place & 3
                column = ((dest // N + dz) & 3) * N + ((dest % N + dx) & 3)
                move(
                    source.at[pl.ds(dest * rows, rows), pl.ds(pl.multiple_of(column * width, width), width)],
                    out.at[dest, pl.ds(0, rows), pl.ds(part * width, width)],
                )
                move(
                    lines.at[pl.ds(part * fold, fold), pl.ds(dest * width, width)],
                    out.at[dest, pl.ds(rows, fold), pl.ds(part * width, width)],
                )
        for copy in copies:
            copy.wait()

    return pl.pallas_call(
        kernel,
        out_shape=jax.ShapeDtypeStruct((blocks, rows + fold, 2 * width), key_value_grad.dtype),
        grid_spec=pltpu.PrefetchScalarGridSpec(
            num_scalar_prefetch=0,
            grid=(1,),
            in_specs=[pl.BlockSpec(memory_space=pl.ANY)] * 2,
            out_specs=pl.BlockSpec(memory_space=pltpu.VMEM),
            scratch_shapes=[pltpu.SemaphoreType.DMA((4 * blocks,))],
        ),
        name="slices_out",
    )(key_value_grad, newline_grad)


CUTS = ((6, 10), (10, 14), (4, 6), (14, 16), (0, 4))


def turn_features(siglip_features, convnext_features):
    rows = siglip_features.shape[0]
    blocks = N * N
    sizes = [siglip_features.shape[1] // blocks, convnext_features.shape[1] // blocks]
    size = sum(sizes)

    def kernel(siglip_ref, convnext_ref, *refs):
        count = 2 * len(CUTS)
        outs, staged, scratch, sems = refs[:count], refs[count:2 * count], refs[2 * count:-1], refs[-1]
        for source, target in zip((siglip_ref, convnext_ref), scratch):
            for i in range(source.shape[1] // 128):
                at = slice(i * 128, (i + 1) * 128)
                target[at] = source[:, at].T.astype(F32)
        first, _ = order_blocks()

        def store(order, place, value):
            for piece, (start, stop) in enumerate(CUTS):
                if start <= place < stop:
                    at = (place - start) * size
                    staged[order * len(CUTS) + piece][at:at + size] = value

        for place in range(blocks):
            value = jnp.concatenate(
                [
                    source[pl.ds(pl.multiple_of(first[place] * n, 8), n)]
                    for source, n in zip(scratch, sizes)
                ],
                axis=0,
            ).astype(BF)
            store(0, place, value)
            store(1, (place % N) * N + place // N, value)
        copies = [pltpu.make_async_copy(staged[i], outs[i], sems.at[i]) for i in range(count)]
        for copy in copies:
            copy.start()
        for copy in copies:
            copy.wait()

    shapes = [
        jax.ShapeDtypeStruct(((stop - start) * size, rows), siglip_features.dtype) for start, stop in CUTS
    ] * 2
    outs = pl.pallas_call(
        kernel,
        out_shape=[pltpu.HBM(shape.shape, shape.dtype) for shape in shapes],
        grid_spec=pltpu.PrefetchScalarGridSpec(
            num_scalar_prefetch=0,
            grid=(1,),
            in_specs=[
                pl.BlockSpec(siglip_features.shape, lambda i: (0, 0)),
                pl.BlockSpec(convnext_features.shape, lambda i: (0, 0)),
            ],
            out_specs=[pl.BlockSpec(memory_space=pltpu.HBM)] * len(shapes),
            scratch_shapes=[pltpu.VMEM(shape.shape, shape.dtype) for shape in shapes]
            + [
                pltpu.VMEM((siglip_features.shape[1], rows), F32),
                pltpu.VMEM((convnext_features.shape[1], rows), F32),
                pltpu.SemaphoreType.DMA((len(shapes),)),
            ],
        ),
        compiler_params=pltpu.CompilerParams(vmem_limit_bytes=32 * 1024 * 1024),
        name="turn_features",
    )(siglip_features, convnext_features)
    return outs[:len(CUTS)], outs[len(CUTS):]


def pick_tiles(received, dests, extra):
    tiles = dests.shape[0]
    width = received.shape[2]
    rows = tiles * TT

    def kernel(dest_ref, source, extra_ref, out, sems):
        names = [dest_ref[j] for j in range(tiles)]
        copies = []
        for j in range(tiles):
            before = jnp.int32(0)
            for i in range(j):
                before = before + (names[i] == names[j]).astype(jnp.int32)
            copy = pltpu.make_async_copy(
                source.at[names[j], pl.ds(pl.multiple_of(before * TT, TT), TT)],
                out.at[pl.ds(j * TT, TT)],
                sems.at[j],
            )
            copy.start()
            copies.append(copy)
        out[rows:] = extra_ref[...]
        for copy in copies:
            copy.wait()

    return pl.pallas_call(
        kernel,
        out_shape=jax.ShapeDtypeStruct((rows + EXTRA, width), received.dtype),
        grid_spec=pltpu.PrefetchScalarGridSpec(
            num_scalar_prefetch=1,
            grid=(1,),
            in_specs=[
                pl.BlockSpec(memory_space=pltpu.HBM),
                pl.BlockSpec((EXTRA, width), lambda i, t: (0, 0)),
            ],
            out_specs=pl.BlockSpec((rows + EXTRA, width), lambda i, t: (0, 0)),
            scratch_shapes=[pltpu.SemaphoreType.DMA((tiles,))],
        ),
        name="pick_tiles",
    )(dests, received, extra)


def step(kernel, name, ins, outs, scratch, copies, limit=24):
    return pl.pallas_call(
        kernel,
        out_shape=[space(shape.shape, shape.dtype) for shape, space in outs],
        grid_spec=pltpu.PrefetchScalarGridSpec(
            num_scalar_prefetch=0,
            grid=(1,),
            in_specs=[pl.BlockSpec(memory_space=space) for _, space in ins],
            out_specs=[pl.BlockSpec(memory_space=space) for _, space in outs],
            scratch_shapes=list(scratch) + [pltpu.SemaphoreType.DMA((copies,))],
        ),
        compiler_params=pltpu.CompilerParams(vmem_limit_bytes=limit * 1024 * 1024),
        name=name,
    )(
        *[array if space is ANY else pltpu.with_memory_space_constraint(array, space) for array, space in ins],
    )


class Copies:
    def __init__(self, sems):
        self.sems, self.count = sems, 0

    def start(self, source, target):
        copy = pltpu.make_async_copy(source, target, self.sems.at[self.count])
        self.count += 1
        copy.start()
        return copy


def down(row):
    return jnp.broadcast_to(row, (128, row.shape[1])).T


CHUNK = 256
FAR = (2, 1, 3)


def tile_step(pieces, projected, key_value_weight, newline_embed):
    wide = pieces[0].shape[1]
    rows = pieces[0].shape[0] - EXTRA
    width = wide // 2
    count = len(pieces)
    blocks = 2 * count
    share = projected.shape[1]
    deep = rows // wide
    half = share // 2
    dtype = pieces[0].dtype

    def kernel(*refs):
        piece_refs = refs[:count]
        proj_hbm, weight_hbm, embed_ref = refs[count:count + 3]
        kept, (grad_hbm, normed_hbm) = refs[count + 3:count + 9], refs[count + 9:count + 11]
        sends, (products_ref, inverse_ref, line_ref) = refs[count + 11:count + 15], refs[count + 15:count + 18]
        sources, proj_ref, weight_ref, first, second, grad_ref, normed_ref, staged, whole, sems = refs[
            count + 18:
        ]
        copies = Copies(sems)
        held = copies.start(piece_refs[0], sources)
        waits = [copies.start(proj_hbm, proj_ref), copies.start(weight_hbm, weight_ref)]
        z, x, core = lax.axis_index("z"), lax.axis_index("x"), lax.axis_index("core")
        y = lax.axis_index("yhi") * 2 + lax.axis_index("ylo")
        extra = jnp.zeros((EXTRA, wide), F32)
        for p, (side, steps) in enumerate([(side, steps) for side in (0, 1) for steps in (0, 1, 3, 2)]):
            if p == 0:
                held.wait()
            source = piece_refs[p] if p else sources
            extra = extra + source[rows:].astype(F32)
            other = (y - steps) & 3
            member = ((other & 1) * 2 + ((core + side) & 1)) * 2 + (other >> 1)
            for part in range(2):
                place = 2 * member + part
                turn = (place & 3) * N + (place >> 2)
                block = ((z + (place & 3)) & 3) * N + ((x + (place >> 2)) & 3)
                value = source[:rows, part * width:(part + 1) * width]
                whole[:, pl.ds(pl.multiple_of(block * width, width), width)] = value
                flipped = value.T
                first[place] = flipped
                second[turn] = flipped
        leaving = [
            copies.start((first, second)[i // 3].at[pl.ds(start, stop - start)], kept[i])
            for i, (start, stop) in enumerate(CUTS[2:] * 2)
        ]
        for i in range(deep):
            squares = extra[i:i + 1] + extra[deep + i:deep + i + 1] + extra[2 * deep + i:2 * deep + i + 1]
            inverse_ref[i * wide:(i + 1) * wide] = lax.rsqrt(down(squares) / D + epsilon)
        line = jnp.sum(
            jnp.sum(extra[3 * deep:3 * deep + 3], axis=0, keepdims=True), axis=1, keepdims=True
        )
        line = embed_ref[...].astype(F32) * lax.rsqrt(line / D + epsilon)
        line_ref[...] = line.astype(BF).astype(F32)
        waits[0].wait()
        for i in range(share // 128):
            at = slice(i * 128, (i + 1) * 128)
            normed_ref[:, at] = (proj_ref[:, at].astype(F32) * inverse_ref[...]).astype(BF)
        leaving.append(copies.start(normed_ref, normed_hbm))
        for i in range(4):
            start, stop = CUTS[i % 2]
            left = (first, second)[i // 2][start:stop].reshape(N * width, rows)
            right = normed_ref[:, (i // 2) * half:(i // 2 + 1) * half]
            staged[i] = jnp.dot(left, right, preferred_element_type=F32).astype(BF)
            leaving.append(copies.start(staged.at[i], sends[i]))
        waits[1].wait()
        products = jnp.zeros((rows, 1), F32)
        for i in range(share // CHUNK):
            at = slice(i * CHUNK, (i + 1) * CHUNK)
            grad = jnp.dot(whole[...], weight_ref[:, at], preferred_element_type=F32).astype(BF)
            grad_ref[:, at] = grad
            leaving.append(copies.start(grad_ref.at[:, at], grad_hbm.at[:, at]))
            products = products + jnp.sum(
                grad.astype(F32) * proj_ref[:, at].astype(F32), axis=1, keepdims=True
            )
        products = jnp.broadcast_to(products, (rows, 128)).T
        products = jnp.concatenate(
            [products[:1, i * 128:(i + 1) * 128] for i in range(rows // 128)]
            + [jnp.zeros((8 - rows // 128, 128), F32)],
            axis=0,
        )
        products_ref[...] = jnp.broadcast_to(products[None], products_ref.shape)
        for copy in leaving:
            copy.wait()

    turned = jax.ShapeDtypeStruct((blocks, width, rows), dtype)
    grad = jax.ShapeDtypeStruct((rows, share), BF)
    outs = step(
        kernel,
        "tile_step",
        [(pieces[0], HBM)] + [(piece, VMEM) for piece in pieces[1:]]
        + [(projected, HBM), (key_value_weight, HBM), (newline_embed, VMEM)],
        [(jax.ShapeDtypeStruct((stop - start, width, rows), dtype), HBM) for start, stop in CUTS[2:]] * 2
        + [
            (grad, HBM),
            (grad, HBM),
        ]
        + [(jax.ShapeDtypeStruct((N * width, half), BF), HBM)] * 4
        + [
            (jax.ShapeDtypeStruct((count, 8, 128), F32), VMEM),
            (jax.ShapeDtypeStruct((rows, 128), F32), VMEM),
            (jax.ShapeDtypeStruct((1, share), F32), VMEM),
        ],
        [
            VMEM(pieces[0].shape, dtype),
            VMEM(projected.shape, BF),
            VMEM(key_value_weight.shape, BF),
            VMEM(turned.shape, dtype),
            VMEM(turned.shape, dtype),
            VMEM(grad.shape, BF),
            VMEM(grad.shape, BF),
            VMEM((4, N * width, half), BF),
            VMEM((rows, wide * count), dtype),
        ],
        count + 13 + share // CHUNK,
    )
    return outs[:6], outs[6:8], outs[8:12], outs[12:]


def x_rest(features, projected_grad, turned, normed):
    rows, share = normed.shape
    half = share // 2
    lefts = list(features) + list(turned)
    arrays = lefts + [projected_grad, normed]
    count = len(lefts)
    tall = [left.size // rows for left in lefts]
    shapes = [jax.ShapeDtypeStruct((height, half), F32) for height in tall]

    def kernel(*refs):
        ins, outs = refs[:count + 2], refs[count + 2:2 * count + 2]
        held, sems = refs[2 * count + 2:-1], refs[-1]
        copies = Copies(sems)
        right_sides = [copies.start(ins[count + i], held[count + i]) for i in range(2)]
        arriving = [copies.start(ins[i], held[i]) for i in range(count)]
        for i in range(count):
            which = i // (count // 2)
            if i % (count // 2) == 0:
                right_sides[which].wait()
            arriving[i].wait()
            order = (i // 3) % 2
            right = held[count + which][:, order * half:(order + 1) * half]
            outs[i][...] = jnp.dot(
                held[i][...].reshape(tall[i], rows), right, preferred_element_type=F32
            )

    outs = step(
        kernel,
        "x_rest",
        [(array, HBM) for array in arrays],
        [(shape, VMEM) for shape in shapes],
        [VMEM(array.shape, BF) for array in arrays],
        count + 2,
        limit=16,
    )
    return outs[:3], outs[3:6], outs[6:9], outs[9:]


def x_first(products, grad, projected, inverse, features1, features2):
    rows, share = grad.shape
    half = share // 2
    size = features1[0].shape[0]

    def kernel(products_ref, grad_ref, proj_ref, inverse_ref, *refs):
        features, out_hbm, sends = refs[:4], refs[4], refs[5:9]
        out, staged, sems = refs[9:]
        copies = Copies(sems)
        total = jnp.sum(products_ref[...], axis=0)
        total = jnp.concatenate([down(total[i:i + 1]) for i in range(rows // 128)], axis=0)
        inv = inverse_ref[...]
        scale = inv * inv * inv * total / D
        for i in range(share // 128):
            at = slice(i * 128, (i + 1) * 128)
            out[:, at] = (
                inv * grad_ref[:, at].astype(F32) - scale * proj_ref[:, at].astype(F32)
            ).astype(BF)
        leaving = [copies.start(out, out_hbm)]
        for i in range(4):
            right = out[:, (i // 2) * half:(i // 2 + 1) * half]
            staged[i] = jnp.dot(features[i][...], right, preferred_element_type=F32).astype(BF)
            leaving.append(copies.start(staged.at[i], sends[i]))
        for copy in leaving:
            copy.wait()

    outs = step(
        kernel,
        "x_first",
        [(products, VMEM), (grad, VMEM), (projected, VMEM), (inverse, VMEM)]
        + [(cut, VMEM) for cut in (features1[0], features1[1], features2[0], features2[1])],
        [(jax.ShapeDtypeStruct((rows, share), BF), HBM)]
        + [(jax.ShapeDtypeStruct((size, half), BF), HBM)] * 4,
        [
            VMEM(grad.shape, BF),
            VMEM((4, size, half), BF),
        ],
        5,
        limit=12,
    )
    return outs[0], outs[1:3], outs[3:5]


def ring_sends(partials, ahead, behind):
    near, far, _ = partials
    half = near.shape[0]
    return (
        (near + ahead[half:].astype(F32)).astype(BF),
        (far + behind[:half].astype(F32)).astype(BF),
    )


def ring_blocks(partials, ahead, behind, ahead2, behind2):
    own = partials[2]
    half = own.shape[0] // 2
    low = own[:half] + behind[half:].astype(F32) + ahead2.astype(F32)
    high = own[half:] + ahead[:half].astype(F32) + behind2.astype(F32)
    size = half // 2
    return low[:size], low[size:], high[:size], high[size:]


def straight(blocks, axis, after=None):
    leaving = [blocks[d].astype(BF) for d in FAR]
    if after is not None:
        leaving[1], after = lax.optimization_barrier((leaving[1], after))
    arrived = [shift(block, axis, N, d) for block, d in zip(leaving, FAR)]
    return blocks[0] + sum(a.astype(F32) for a in arrived), arrived[1]


def local(
    siglip_features,
    convnext_features,
    siglip_projection,
    convnext_projection,
    newline_embed,
    key_value_weight,
    tile_rank,
    row_end,
    key_value_grad,
    newline_grad,
):
    blocks = N * N
    z, x = lax.axis_index("z"), lax.axis_index("x")
    my_rank = z * N + x
    tiles = tile_rank.shape[0]
    per_device = tiles // blocks
    rows = siglip_features.shape[0]
    share = siglip_projection.shape[1]
    half = share // 2
    kv_rows = key_value_weight.shape[0] // blocks
    sig_rows = siglip_features.shape[1] // blocks
    conv_rows = convnext_features.shape[1] // blocks

    dest_rank = tile_rank.reshape(tiles)
    mine = lax.dynamic_slice_in_dim(dest_rank, my_rank * per_device, per_device)
    outgoing = slices_out(key_value_grad, newline_grad)
    received = lax.all_to_all(outgoing, DP, split_axis=0, concat_axis=0, tiled=True)

    projected = (
        jnp.dot(siglip_features, siglip_projection, preferred_element_type=F32)
        + jnp.dot(convnext_features, convnext_projection, preferred_element_type=F32)
    ).astype(BF)
    proj_values = projected.astype(F32)
    line_vector = newline_embed.astype(F32)
    wide = received.shape[2]
    deep = rows // wide
    squares = jnp.sum(proj_values * proj_values, axis=1).reshape(deep, wide)
    line_squares = jnp.sum((line_vector * line_vector).reshape(share // wide, wide), axis=0)[None]
    statistics = extra_rows(thirds(squares) + thirds(line_squares))

    features1, features2 = turn_features(siglip_features, convnext_features)
    x_rows = sig_rows + conv_rows
    received, statistics, features1, features2 = lax.optimization_barrier(
        (received, statistics, features1, features2)
    )
    own = pick_tiles(received, mine, statistics)
    own, received, dest_rank, row_end = lax.optimization_barrier((own, received, dest_rank, row_end))
    ring = [own] + [shift_y(own, s) for s in (1, 3, 2)]
    pieces = ring + [shift(piece, "core", 2, 1) for piece in ring]

    onehot = (dest_rank[:, None] == jnp.arange(blocks, dtype=jnp.int32)[None, :]).astype(jnp.int32)
    grouped = onehot.reshape(blocks, per_device, blocks)
    before = jnp.cumsum(grouped, axis=1) - grouped
    slot_place = jnp.sum(before * grouped, axis=2).reshape(tiles)
    slot = (jnp.arange(tiles, dtype=jnp.int32) // per_device) * CAP + slot_place
    slot_index = dest_rank * (blocks * CAP) + slot
    mask = jnp.sum(
        (
            (slot_index[:, None] == jnp.arange(blocks * blocks * CAP, dtype=jnp.int32)[None, :])
            & (row_end[:, None] == 1)
        ).astype(F32),
        axis=0,
    ).astype(BF)
    mask = mask.reshape(blocks, 2, blocks)
    line_rows = received[:, CAP * TT:]
    line_total = sum(
        jnp.dot(
            mask[:, part].reshape(1, blocks * blocks),
            line_rows[:, :, part * kv_rows:(part + 1) * kv_rows].reshape(blocks * blocks, kv_rows),
            preferred_element_type=F32,
        )
        for part in range(2)
    )
    line_total = jnp.broadcast_to(line_total, (kv_rows, kv_rows)).T

    newline_embed, line_total = lax.optimization_barrier((newline_embed, line_total))
    turned, (normed_grad, normed), kv_sends, (products, inverse, line_normed) = tile_step(
        pieces, projected, key_value_weight, newline_embed.reshape(1, share)
    )
    products = lax.all_to_all(products, ("ylo", "core", "yhi"), split_axis=0, concat_axis=0, tiled=True)

    def both_ways(pair, axis):
        return shift(pair[0], axis, N, 1), shift(pair[1], axis, N, 3)

    kv_in = [both_ways(kv_sends[:2], "x"), both_ways(kv_sends[2:], "z")]
    projected_grad, x_send0, x_send1 = x_first(
        products, normed_grad, projected, inverse, features1, features2
    )
    x_in = [both_ways(x_send0, "x"), both_ways(x_send1, "z")]
    kv_in, projected_grad = lax.optimization_barrier((kv_in, projected_grad))
    parts = x_rest(list(features1[2:]) + list(features2[2:]), projected_grad, turned, normed)
    results, after = [], None
    for i, first, second in ((1, "z", "x"), (0, "x", "z")):
        x_parts, kv_parts = parts[i], parts[2 + i]
        sends = [
            jnp.concatenate(pair, axis=0)
            for pair in zip(ring_sends(x_parts, *x_in[i]), ring_sends(kv_parts, *kv_in[i]))
        ]
        ahead, behind = both_ways(sends, first)
        size = x_parts[0].shape[0]
        x_blocks = ring_blocks(x_parts, *x_in[i], ahead[:size], behind[:size])
        kv_blocks = ring_blocks(kv_parts, *kv_in[i], ahead[size:], behind[size:])
        result, after = straight(
            [jnp.concatenate(pair, axis=0) for pair in zip(x_blocks, kv_blocks)], second, after
        )
        results.insert(0, result)
    siglip_result, convnext_result, kv_result = [
        jnp.concatenate([result[start:stop] for result in results], axis=1)
        for start, stop in ((0, sig_rows), (sig_rows, x_rows), (x_rows, x_rows + kv_rows))
    ]
    kv_result = kv_result + line_total[:, :1] * line_normed
    return siglip_result, convnext_result, kv_result


def solution(mesh):
    fine = Mesh(mesh.devices.reshape(2, 2, N, N, 2), ("ylo", "core", "z", "x", "yhi"))
    wide = ("ylo", "core", "yhi")
    in_specs = (
        P(DP, None),
        P(DP, None),
        P(None, wide),
        P(None, wide),
        P(wide),
        P(None, wide),
        P(),
        P(),
        P(DP, None),
        P(DP, None),
    )
    out_specs = (P(DP, wide), P(DP, wide), P(DP, wide))
    return jax.shard_map(local, mesh=fine, in_specs=in_specs, out_specs=out_specs, check_vma=False)
```
